32 devices in a mesh: grp: 4 (over x, core), slab: 8 (over z, y).
Axes of the slice: x: 2, y: 2, z: 4, core: 2. Of those that a mesh axis runs over, the one named last changes fastest.
Arguments:
- theta: float32 [4, 128, 64, 256], P('grp', 'slab'), may hold values from -6 to 6
- register: float32 [4, 128, 64, 256], P('grp', 'slab'), may hold values from -6 to 6
- velocity: bfloat16 [3, 64, 32, 128], P(None, 'slab', 'grp'), may hold values from -6 to 6
- diffusivity: float32 [4], P('grp'), may hold values from 0.05 to 0.5
Outputs:
- theta_new: float32 [4, 128, 64, 256], P('grp', 'slab')
- register_new: float32 [4, 128, 64, 256], P('grp', 'slab')
The draws below stay inside these ranges and needn't reach their ends.
All inputs are finite; a program needn't handle non-finite values.
Results may differ from the reference program's by a relative error of at most 0.0014.
Values may be sent and summed in bfloat16 or wider, within the bound.
No kernel may reach another device: no remote copies, remote signals or barrier semaphores. Data moves between devices by JAX's collectives and lax.ppermute only.
A program may use at most 64 MiB of HBM per device.

```python
import math
import jax
import jax.numpy as jnp
from jax import lax

PX = 16
BLK = 32
NYF = 64
NZF = 256
NXF = 128
NXC = 64
NYC = 32
NZC = 128
SCALARS = 4


def block_levels(own_key, shape, cuts, smallest, largest):
    gain, own = 1.0, jax.random.fold_in(own_key, 6)
    for axis_at, parts in cuts:
        heights = jnp.exp(jax.random.uniform(jax.random.fold_in(own, axis_at), (parts,), jnp.float32, smallest / len(cuts), largest / len(cuts)))
        gain = gain * jnp.repeat(heights, shape[axis_at] // parts).reshape([-1 if axis == axis_at else 1 for axis in range(len(shape))])
    return gain


def noise(stream_key, dims, width, limit, cuts=(), kind=jnp.bfloat16):
    drawn = jax.random.normal(stream_key, dims, jnp.float32) * width
    if len(cuts) > 0:
        drawn = block_levels(stream_key, dims, cuts, -0.22, 0.18) * drawn
    return jnp.clip(drawn, min=-limit, max=limit).astype(kind)


def setup_inputs(seed: int = 0) -> dict:
    arg_keys = jax.random.split(jax.random.key(seed), 5)
    return {
        "theta": noise(arg_keys[0], (SCALARS, NXF, NYF, NZF), 1.0, 6.0, ((0, 4), (1, 8)), jnp.float32),
        "register": noise(arg_keys[1], (SCALARS, NXF, NYF, NZF), 1.0, 6.0, ((0, 4), (1, 8)), jnp.float32),
        "velocity": noise(arg_keys[2], (3, NXC, NYC, NZC), 1.0, 6.0, ((1, 8), (2, 4))),
        "diffusivity": jnp.clip(jnp.exp(math.log(0.5) - 2.3025851 * jax.random.uniform(arg_keys[3], (SCALARS,), jnp.float32) ** block_levels(arg_keys[3], (SCALARS,), ((0, 4),), -0.2, 0.2)), 0.05, 0.5),
    }


ALPHA = 4.0 / 9.0
BETA = 1.0 / 36.0
COEF_A = 40.0 / 27.0
COEF_B = 25.0 / 54.0
RK_A = -5.0 / 9.0
RK_B = 15.0 / 16.0
STEP = 0.2

def band_matrices(count, periodic):
    rows = jnp.arange(count)[:, None]
    cols = jnp.arange(count)[None, :]
    offset = cols - rows
    if periodic:
        offset = (offset + count // 2) % count - count // 2
    one = jnp.float32(1.0)
    zero = jnp.float32(0.0)
    lhs = jnp.where(offset == 0, one, zero) + ALPHA * jnp.where(jnp.abs(offset) == 1, one, zero) + BETA * jnp.where(jnp.abs(offset) == 2, one, zero)
    rhs = 0.5 * COEF_A * (jnp.where(offset == 1, one, zero) - jnp.where(offset == -1, one, zero)) + 0.25 * COEF_B * (jnp.where(offset == 2, one, zero) - jnp.where(offset == -2, one, zero))
    return (lhs, rhs)

def block_inverse(count):
    lhs, rhs = band_matrices(count, False)
    factor = jnp.linalg.cholesky(lhs)
    return jax.scipy.linalg.cho_solve((factor, True), jnp.eye(count, dtype=lhs.dtype))

def blocked_operator(count, block):
    lhs, rhs = band_matrices(count, True)
    inverse = block_inverse(block)
    diagonal = jnp.kron(jnp.eye(count // block, dtype=jnp.float32), inverse)
    return jnp.dot(diagonal, rhs, precision=lax.Precision.HIGHEST)

def wrap_pad(field, axis):
    count = field.shape[axis]
    left = lax.slice_in_dim(field, count - 2, count, axis=axis)
    right = lax.slice_in_dim(field, 0, 2, axis=axis)
    return jnp.concatenate([left, field, right], axis=axis)

def refine(padded, axis, count):

    def taken(shift):
        return lax.slice_in_dim(padded, 2 + shift, 2 + shift + count, axis=axis)
    even = -0.0390625 * taken(-2) + 0.2734375 * taken(-1) + 0.8203125 * taken(0) - 0.0546875 * taken(1)
    odd = -0.0546875 * taken(-1) + 0.8203125 * taken(0) + 0.2734375 * taken(1) - 0.0390625 * taken(2)
    stacked = jnp.stack([even, odd], axis=axis + 1)
    shape = list(even.shape)
    shape[axis] = 2 * count
    return stacked.reshape(shape)

def x_derivative(field, inverse):
    rhs = 0.5 * COEF_A * (jnp.roll(field, -1, 0) - jnp.roll(field, 1, 0)) + 0.25 * COEF_B * (jnp.roll(field, -2, 0) - jnp.roll(field, 2, 0))
    blocks = rhs.reshape((-1, PX) + field.shape[1:])
    out = jnp.einsum('ij,bjyz->biyz', inverse, blocks, precision=lax.Precision.HIGHEST)
    return out.reshape(field.shape)

def y_derivative(field, operator):
    return jnp.einsum('ij,xjz->xiz', operator, field, precision=lax.Precision.HIGHEST)

def z_derivative(field, operator):
    return jnp.einsum('ij,xyj->xyi', operator, field, precision=lax.Precision.HIGHEST)

def reference(theta, register, velocity, diffusivity):
    coarse = velocity.astype(jnp.float32)
    flow = refine(wrap_pad(coarse, 1), 1, coarse.shape[1])
    flow = refine(wrap_pad(flow, 2), 2, flow.shape[2])
    flow = refine(wrap_pad(flow, 3), 3, flow.shape[3])
    inverse = block_inverse(PX)
    oper_y = blocked_operator(NYF, BLK)
    oper_z = blocked_operator(NZF, BLK)

    def one_scalar(items):
        field, saved, kappa = items
        grad_x = x_derivative(field, inverse)
        grad_y = y_derivative(field, oper_y)
        grad_z = z_derivative(field, oper_z)
        flux_x = flow[0] * field - kappa * grad_x
        flux_y = flow[1] * field - kappa * grad_y
        flux_z = flow[2] * field - kappa * grad_z
        rate = -(x_derivative(flux_x, inverse) + y_derivative(flux_y, oper_y) + z_derivative(flux_z, oper_z))
        new_saved = RK_A * saved + STEP * rate
        return (field + RK_B * new_saved, new_saved)
    theta_new, register_new = lax.map(one_scalar, (theta, register, diffusivity))
    return (theta_new, register_new)
```

```python
import jax
import jax.numpy as jnp
import numpy as np
from jax import lax
from jax.experimental import pallas as pl
from jax.experimental.pallas import tpu as pltpu
from jax.sharding import PartitionSpec as P

BLK = 32
ALPHA = 4.0 / 9.0
BETA = 1.0 / 36.0
COEF_A = 40.0 / 27.0
COEF_B = 25.0 / 54.0
RK_A = -5.0 / 9.0
RK_B = 15.0 / 16.0
STEP = 0.2
EVEN = (-0.0390625, 0.2734375, 0.8203125, -0.0546875)
ODD = (-0.0546875, 0.8203125, 0.2734375, -0.0390625)
MXU = 256


def band(count):
    eye = lambda k: np.eye(count, k=k)
    return eye(0) + ALPHA * (eye(1) + eye(-1)) + BETA * (eye(2) + eye(-2))


def blocked_operator(count, block):
    rhs = np.zeros((count, count))
    for i in range(count):
        for shift, coef in ((1, COEF_A / 2), (-1, -COEF_A / 2), (2, COEF_B / 4), (-2, -COEF_B / 4)):
            rhs[i, (i + shift) % count] += coef
    return np.kron(np.eye(count // block), np.linalg.inv(band(block))) @ rhs


def refine_operator(count):
    out = np.zeros((2 * count, count))
    for k in range(count):
        for t in range(4):
            out[2 * k, (k - 2 + t) % count] += EVEN[t]
            out[2 * k + 1, (k - 1 + t) % count] += ODD[t]
    return out


def split(x):
    hi = x.astype(jnp.bfloat16)
    return hi, (x - hi.astype(jnp.float32)).astype(jnp.bfloat16)


def host_split(x):
    x = jnp.asarray(np.asarray(x, np.float32))
    return jnp.stack(split(x))


def dot(a, b):
    return jnp.dot(a, b, preferred_element_type=jnp.float32)


def dot3(a, b):
    return dot(a[0], b[0]) + (dot(a[0], b[1]) + dot(a[1], b[0]))


def banded_lu(count):
    m = band(count)
    for k in range(count):
        for i in range(k + 1, min(k + 3, count)):
            m[i, k] /= m[k, k]
            m[i, k + 1 : min(k + 3, count)] -= m[i, k] * m[k, k + 1 : min(k + 3, count)]
    return m


def x_derivative(get, put, work, planes):
    m = banded_lu(planes)
    ratio = (COEF_B / 4) / (COEF_A / 2)
    y1 = y2 = None
    for i in range(planes):
        y = (get(i + 1) - get(i - 1)) + ratio * (get(i + 2) - get(i - 2))
        if i >= 1:
            y = y - float(m[i, i - 1]) * y1
        if i >= 2:
            y = y - float(m[i, i - 2]) * y2
        work[i] = y
        y1, y2 = y, y1
    x1 = x2 = None
    for i in reversed(range(planes)):
        inv = 1.0 / m[i, i]
        x = work[i] * float(inv * COEF_A / 2)
        if i + 1 < planes:
            x = x - float(m[i, i + 1] * inv) * x1
        if i + 2 < planes:
            x = x - float(m[i, i + 2] * inv) * x2
        put(i, x)
        x1, x2 = x, x1


def second_kernel(th, ky2, kz2, out):
    planes, ny, nz = th.shape
    per = ky2.shape[1] // ny
    for g in range(planes // per):
        x = split(th[g * per : (g + 1) * per].reshape(per * ny, nz))
        value = dot3(ky2, x) + dot3(x, kz2)
        out[g * per : (g + 1) * per] = value.reshape(per, ny, nz)


def first_kernel(part, th, tl, tr, *refs):
    parts = refs[: -5]
    gx, vel, tail, head, work = refs[-5:]
    planes, ny, nz = th.shape
    ngrp = len(parts)
    rows, nzc = parts[0].shape[2:]
    nyc = rows * ngrp
    coarse = planes // 2
    for s in range(ngrp):
        at = pl.multiple_of(((part[0] + (ngrp - s)) % ngrp) * rows, rows)
        vel[:, :, pl.ds(at, rows), :] = parts[s][...].astype(jnp.float32)

    def get(p):
        if p < 0:
            return tl[p + 2].astype(jnp.float32)
        if p >= planes:
            return tr[p - planes].astype(jnp.float32)
        return th[p]

    def put(i, value):
        gx[i] = value
        if i < 2:
            head[i] = value.astype(jnp.bfloat16)
        if i >= planes - 2:
            tail[i - (planes - 2)] = value.astype(jnp.bfloat16)

    x_derivative(get, put, work, planes)
    for q in range(8):
        c, k = ((0, 0), (0, 1), (0, 2), (1, 0), (1, 1), (2, 0), (2, 1), (2, 1))[q]
        count = 3 if c == 0 else 2
        at = (2 + q // 4, slice(nyc * (q // 2 % 2), nyc * (q // 2 % 2 + 1)), slice(nzc * (q % 2), nzc * (q % 2 + 1)))
        head[at] = vel[c, k].astype(jnp.bfloat16)
        tail[at] = vel[c, coarse - count + k].astype(jnp.bfloat16)


def final_kernel(kap, th, reg, lap, gx, tl, tr, pay_l, pay_r, vel, ky, kz, ry, rz, new, saved, flux, acc):
    planes, ny, nz = th.shape
    nyc, nzc = vel.shape[2:]
    coarse = planes // 2
    per = ky.shape[1] // ny
    kappa = kap[0]

    def slot(pay, q):
        return pay[2 + q // 4, nyc * (q // 2 % 2) : nyc * (q // 2 % 2 + 1), nzc * (q % 2) : nzc * (q % 2 + 1)].astype(jnp.float32)

    def plane(c, k):
        first, count = ((0, 3), (3, 2), (5, 2))[c]
        if k < 0:
            return slot(pay_l, first + count + k)
        if k >= coarse:
            return slot(pay_r, first + k - coarse)
        return vel[c, k]

    def fine(c, p):
        k = p // 2
        coefs, start = (EVEN, k - 2) if p % 2 == 0 else (ODD, k - 1)
        total = coefs[0] * plane(c, start)
        for t in range(1, 4):
            total = total + coefs[t] * plane(c, start + t)
        return total

    def flow(c, p):
        x = split(jnp.concatenate([fine(c, p + i) for i in range(per)], axis=0))
        z = split(dot(x[0], rz[...]) + dot(x[1], rz[...]))
        return dot(ry[...], z[0]) + dot(ry[...], z[1])

    for g in range(planes // per):
        at = slice(g * per, (g + 1) * per)
        x = th[at].reshape(per * ny, nz)
        fy = split(flow(1, g * per) * x)
        fz = split(flow(2, g * per) * x)
        acc[at] = (dot3(ky, fy) + dot3(fz, kz)).reshape(per, ny, nz) - kappa * lap[at]
    for g in range((planes + 4) // per):
        f = flow(0, g * per - 2).reshape(per, ny, nz)
        for i in range(per):
            p = g * per - 2 + i
            if p < 0:
                t, d = tl[p + 2].astype(jnp.float32), pay_l[p + 2].astype(jnp.float32)
            elif p >= planes:
                t, d = tr[p - planes].astype(jnp.float32), pay_r[p - planes].astype(jnp.float32)
            else:
                t, d = th[p], gx[p]
            flux[p + 2] = f[i] * t - kappa * d

    def put(i, value):
        kept = RK_A * reg[i] - STEP * (value + acc[i])
        saved[i] = kept
        new[i] = th[i] + RK_B * kept

    x_derivative(lambda p: flux[p + 2], put, saved, planes)


def shards(theta, register, velocity, diffusivity):
    planes, ny, nz = theta.shape[1:]
    nslab, ngrp = lax.axis_size("slab"), lax.axis_size("grp")
    nyc, nzc = ny // 2, nz // 2
    per = max(1, MXU // ny)
    f32, bf16 = jnp.float32, jnp.bfloat16
    up = [(i, (i + 1) % nslab) for i in range(nslab)]
    down = [((i + 1) % nslab, i) for i in range(nslab)]
    op_y, op_z = blocked_operator(ny, BLK), blocked_operator(nz, BLK)
    eye = np.eye(per)
    ky2, kz2 = host_split(np.kron(eye, op_y @ op_y)), host_split((op_z @ op_z).T)
    ky, kz = host_split(np.kron(eye, op_y)), host_split(op_z.T)
    ry = jnp.asarray(np.kron(eye, refine_operator(nyc)), bf16)
    rz = jnp.asarray(refine_operator(nzc).T, bf16)

    field, saved = theta[0], register[0]
    head = field[:2].astype(bf16)
    tail = field[planes - 2 :].astype(bf16)
    left = lax.ppermute(tail, "slab", up)
    right = lax.ppermute(head, "slab", down)
    parts = [velocity]
    for s in range(1, ngrp):
        parts.append(lax.ppermute(velocity, "grp", [(i, (i + s) % ngrp) for i in range(ngrp)]))
    full = jax.ShapeDtypeStruct((planes, ny, nz), f32)
    vmem = pl.BlockSpec(memory_space=pltpu.VMEM)
    smem = pl.BlockSpec(memory_space=pltpu.SMEM)
    params = pltpu.CompilerParams(vmem_limit_bytes=30 * 1024 * 1024)
    lap = pl.pallas_call(
        second_kernel, out_shape=full, in_specs=[vmem] * 3, out_specs=vmem, compiler_params=params, name="second"
    )(field, ky2, kz2)
    part = lax.axis_index("grp").astype(jnp.int32)[None]
    pay = jax.ShapeDtypeStruct((4, ny, nz), bf16)
    gx, vel, tail, head = pl.pallas_call(
        first_kernel,
        out_shape=(full, jax.ShapeDtypeStruct((3, planes // 2, nyc, nzc), f32), pay, pay),
        in_specs=[smem] + [vmem] * (3 + ngrp),
        out_specs=(vmem,) * 4,
        scratch_shapes=[pltpu.VMEM((planes, ny, nz), f32)],
        compiler_params=params,
        name="first",
    )(part, field, left, right, *parts)
    pay_l = lax.ppermute(tail, "slab", up)
    pay_r = lax.ppermute(head, "slab", down)
    new, kept = pl.pallas_call(
        final_kernel,
        out_shape=(full, full),
        in_specs=[smem] + [vmem] * 13,
        out_specs=(vmem,) * 2,
        scratch_shapes=[pltpu.VMEM((planes + 4, ny, nz), f32), pltpu.VMEM((planes, ny, nz), f32)],
        compiler_params=params,
        name="final",
    )(diffusivity, field, saved, lap, gx, left, right, pay_l, pay_r, vel, ky, kz, ry, rz)
    return (new[None], kept[None])


def solution(mesh):
    in_specs = (
        P("grp", "slab", None, None),
        P("grp", "slab", None, None),
        P(None, "slab", "grp", None),
        P("grp"),
    )
    out_specs = (P("grp", "slab", None, None), P("grp", "slab", None, None))
    return jax.shard_map(shards, mesh=mesh, in_specs=in_specs, out_specs=out_specs, check_vma=False)
```

```python
import jax
import jax.numpy as jnp
import numpy as np
from jax import lax
from jax.experimental import pallas as pl
from jax.experimental.pallas import tpu as pltpu
from jax.sharding import PartitionSpec as P

BLK = 32
ALPHA = 4.0 / 9.0
BETA = 1.0 / 36.0
COEF_A = 40.0 / 27.0
COEF_B = 25.0 / 54.0
RK_A = -5.0 / 9.0
RK_B = 15.0 / 16.0
STEP = 0.2
EVEN = (-0.0390625, 0.2734375, 0.8203125, -0.0546875)
ODD = (-0.0546875, 0.8203125, 0.2734375, -0.0390625)
MXU = 256


def band(count):
    eye = lambda k: np.eye(count, k=k)
    return eye(0) + ALPHA * (eye(1) + eye(-1)) + BETA * (eye(2) + eye(-2))


def blocked_operator(count, block):
    rhs = np.zeros((count, count))
    for i in range(count):
        for shift, coef in ((1, COEF_A / 2), (-1, -COEF_A / 2), (2, COEF_B / 4), (-2, -COEF_B / 4)):
            rhs[i, (i + shift) % count] += coef
    return np.kron(np.eye(count // block), np.linalg.inv(band(block))) @ rhs


def refine_operator(count):
    out = np.zeros((2 * count, count))
    for k in range(count):
        for t in range(4):
            out[2 * k, (k - 2 + t) % count] += EVEN[t]
            out[2 * k + 1, (k - 1 + t) % count] += ODD[t]
    return out


def split(x):
    hi = x.astype(jnp.bfloat16)
    return hi, (x - hi.astype(jnp.float32)).astype(jnp.bfloat16)


def host_split(x):
    x = jnp.asarray(np.asarray(x, np.float32))
    return jnp.stack(split(x))


def dot(a, b):
    return jnp.dot(a, b, preferred_element_type=jnp.float32)


def dot3(a, b):
    return dot(a[0], b[0]) + (dot(a[0], b[1]) + dot(a[1], b[0]))


def banded_lu(count):
    m = band(count)
    for k in range(count):
        for i in range(k + 1, min(k + 3, count)):
            m[i, k] /= m[k, k]
            m[i, k + 1 : min(k + 3, count)] -= m[i, k] * m[k, k + 1 : min(k + 3, count)]
    return m


def x_derivative(get, put, work, planes):
    m = banded_lu(planes)
    ratio = (COEF_B / 4) / (COEF_A / 2)
    y1 = y2 = None
    for i in range(planes):
        y = (get(i + 1) - get(i - 1)) + ratio * (get(i + 2) - get(i - 2))
        if i >= 1:
            y = y - float(m[i, i - 1]) * y1
        if i >= 2:
            y = y - float(m[i, i - 2]) * y2
        work[i] = y
        y1, y2 = y, y1
    x1 = x2 = None
    for i in reversed(range(planes)):
        inv = 1.0 / m[i, i]
        x = work[i] * float(inv * COEF_A / 2)
        if i + 1 < planes:
            x = x - float(m[i, i + 1] * inv) * x1
        if i + 2 < planes:
            x = x - float(m[i, i + 2] * inv) * x2
        put(i, x)
        x1, x2 = x, x1


SLOTS = ((0, 0), (0, 1), (0, 2), (1, 0), (1, 1), (2, 0), (2, 1))
FIRST, COUNT = (0, 3, 5), (3, 2, 2)


def pack_kernel(low, high, vel, head, tail):
    ny, nz = low.shape[2:]
    coarse, rows, nzc = vel.shape[1:]
    for out, edge, upper in ((head, low, False), (tail, high, True)):
        out[: 2 * ny] = edge[0].reshape(2 * ny, nz).astype(jnp.bfloat16)
        for q in range(8):
            c, k = SLOTS[min(q, 6)]
            k = coarse - COUNT[c] + k if upper else k
            top = 2 * ny + rows * (q // 2)
            out[top : top + rows, nzc * (q % 2) : nzc * (q % 2 + 1)] = vel[c, k]


def padded(th, tl, tr):
    planes, ny = th.shape[:2]

    def get(p):
        if p < 0:
            return tl[ny * (p + 2) : ny * (p + 3)].astype(jnp.float32)
        if p >= planes:
            return tr[ny * (p - planes) : ny * (p - planes + 1)].astype(jnp.float32)
        return th[p]

    return get


def first_kernel(th, tl, tr, gx, halo, tail, head, work):
    planes, ny, nz = th.shape

    def put(i, value):
        gx[i] = value
        if i < 2:
            head[i] = value.astype(jnp.bfloat16)
        if i >= planes - 2:
            tail[i - (planes - 2)] = value.astype(jnp.bfloat16)

    halo[0] = tl[2 * ny :]
    halo[1] = tr[2 * ny :]
    x_derivative(padded(th, tl, tr), put, work, planes)


def flow_of(vel, halo, ry, rz):
    ngrp, _, coarse, rows, nzc = vel.shape

    def plane(c, k):
        if 0 <= k < coarse:
            got = [vel[g, c, k] for g in range(ngrp)]
        else:
            q = FIRST[c] + (COUNT[c] + k if k < 0 else k - coarse)
            top = rows * (q // 2)
            side = 0 if k < 0 else 1
            got = [halo[g, side, top : top + rows, nzc * (q % 2) : nzc * (q % 2 + 1)] for g in range(ngrp)]
        return jnp.concatenate([v.astype(jnp.float32) for v in got], axis=0)

    def fine(c, p):
        k = p // 2
        coefs, start = (EVEN, k - 2) if p % 2 == 0 else (ODD, k - 1)
        total = coefs[0] * plane(c, start)
        for t in range(1, 4):
            total = total + coefs[t] * plane(c, start + t)
        return total

    def flow(c, which):
        x = split(jnp.concatenate([fine(c, p) for p in which], axis=0))
        z = split(dot(x[0], rz[...]) + dot(x[1], rz[...]))
        return dot(ry[...], z[0]) + dot(ry[...], z[1])

    return flow


def is_inner(g, per, planes):
    return g * per >= 4 and (g + 1) * per <= planes - 4


def cross(flow, th, ky, kz, g, per):
    ny, nz = th.shape[1:]
    which = range(g * per, (g + 1) * per)
    x = th[g * per : (g + 1) * per].reshape(per * ny, nz)
    fy = split(flow(1, which) * x)
    fz = split(flow(2, which) * x)
    return (dot3(ky, fy) + dot3(fz, kz)).reshape(per, ny, nz)


def inner_kernel(kap, th, gx, vel, ky, kz, ky2, kz2, ry, rz, acc, flux):
    planes, ny, nz = th.shape
    per = ky.shape[1] // ny
    kappa = kap[0]
    flow = flow_of(vel, None, ry, rz)
    for g in range(planes // per):
        at = slice(g * per, (g + 1) * per)
        x = split(th[at].reshape(per * ny, nz))
        value = -kappa * (dot3(ky2, x) + dot3(x, kz2)).reshape(per, ny, nz)
        if is_inner(g, per, planes):
            value = value + cross(flow, th, ky, kz, g, per)
            flux[at] = flow(0, range(g * per, (g + 1) * per)).reshape(per, ny, nz) * th[at] - kappa * gx[at]
        acc[at] = value


def final_kernel(kap, th, reg, part, inner, gx, tl, tr, gl, gr, vel, halo, ky, kz, ry, rz, new, saved, flux, acc):
    planes, ny, nz = th.shape
    per = ky.shape[1] // ny
    kappa = kap[0]
    flow = flow_of(vel, halo, ry, rz)
    get = padded(th, tl, tr)
    outer = [g for g in range(planes // per) if not is_inner(g, per, planes)]
    for g in outer:
        acc[g * per : (g + 1) * per] = cross(flow, th, ky, kz, g, per) + part[g * per : (g + 1) * per]
    todo = [p for p in range(-2, planes + 2) if not is_inner(p // per, per, planes)]
    for start in range(0, len(todo), per):
        which = todo[start : start + per]
        f = flow(0, which + which[:1] * (per - len(which))).reshape(per, ny, nz)
        for i, p in enumerate(which):
            if p < 0:
                d = gl[p + 2].astype(jnp.float32)
            elif p >= planes:
                d = gr[p - planes].astype(jnp.float32)
            else:
                d = gx[p]
            flux[p + 2] = f[i] * get(p) - kappa * d

    def flux_at(p):
        return inner[p] if is_inner(p // per, per, planes) else flux[p + 2]

    def put(i, value):
        rest = part[i] if is_inner(i // per, per, planes) else acc[i]
        kept = RK_A * reg[i] - STEP * (value + rest)
        saved[i] = kept
        new[i] = th[i] + RK_B * kept

    x_derivative(flux_at, put, saved, planes)


def shards(theta, register, velocity, diffusivity):
    planes, ny, nz = theta.shape[1:]
    nslab, ngrp = lax.axis_size("slab"), lax.axis_size("grp")
    nyc, nzc = ny // 2, nz // 2
    per = max(1, MXU // ny)
    f32, bf16 = jnp.float32, jnp.bfloat16
    up = [(i, (i + 1) % nslab) for i in range(nslab)]
    down = [((i + 1) % nslab, i) for i in range(nslab)]
    op_y, op_z = blocked_operator(ny, BLK), blocked_operator(nz, BLK)
    eye = np.eye(per)
    ky2, kz2 = host_split(np.kron(eye, op_y @ op_y)), host_split((op_z @ op_z).T)
    ky, kz = host_split(np.kron(eye, op_y)), host_split(op_z.T)
    ry = jnp.asarray(np.kron(eye, refine_operator(nyc)), bf16)
    rz = jnp.asarray(refine_operator(nzc).T, bf16)

    field, saved = theta[0], register[0]
    rows, coarse = velocity.shape[2], planes // 2
    full = jax.ShapeDtypeStruct((planes, ny, nz), f32)
    edge = jax.ShapeDtypeStruct((2, ny, nz), bf16)
    packed = jax.ShapeDtypeStruct((2 * ny + 4 * rows, nz), bf16)
    vmem = pl.BlockSpec(memory_space=pltpu.VMEM)
    smem = pl.BlockSpec(memory_space=pltpu.SMEM)
    params = pltpu.CompilerParams(vmem_limit_bytes=30 * 1024 * 1024)

    whole = lambda shape: pl.BlockSpec(shape, lambda i: (0,) * len(shape))
    head, tail = pl.pallas_call(
        pack_kernel,
        out_shape=(packed, packed),
        grid=(1,),
        in_specs=[
            pl.BlockSpec((1, 2, ny, nz), lambda i: (0, 0, 0, 0)),
            pl.BlockSpec((1, 2, ny, nz), lambda i: (0, planes // 2 - 1, 0, 0)),
            whole(velocity.shape),
        ],
        out_specs=(whole(packed.shape),) * 2,
        name="pack",
    )(theta, theta, velocity)
    left = lax.ppermute(tail, "slab", up)
    right = lax.ppermute(head, "slab", down)
    vel = lax.all_gather(velocity, "grp", axis=0, tiled=False)
    gx, halo, tail, head = pl.pallas_call(
        first_kernel,
        out_shape=(full, jax.ShapeDtypeStruct((2, 4 * rows, nz), bf16), edge, edge),
        in_specs=[vmem] * 3,
        out_specs=(vmem,) * 4,
        scratch_shapes=[pltpu.VMEM((planes, ny, nz), f32)],
        compiler_params=params,
        name="first",
    )(field, left, right)
    grad_l = lax.ppermute(tail, "slab", up)
    grad_r = lax.ppermute(head, "slab", down)
    halo = lax.all_gather(halo, "grp", axis=0, tiled=False)
    acc, inner = pl.pallas_call(
        inner_kernel,
        out_shape=(full, full),
        in_specs=[smem] + [vmem] * 9,
        out_specs=(vmem,) * 2,
        compiler_params=params,
        name="inner",
    )(diffusivity, field, gx, vel, ky, kz, ky2, kz2, ry, rz)
    new, kept = pl.pallas_call(
        final_kernel,
        out_shape=(full, full),
        in_specs=[smem] + [vmem] * 15,
        out_specs=(vmem,) * 2,
        scratch_shapes=[pltpu.VMEM((planes + 4, ny, nz), f32), pltpu.VMEM((planes, ny, nz), f32)],
        compiler_params=params,
        name="final",
    )(diffusivity, field, saved, acc, inner, gx, left, right, grad_l, grad_r, vel, halo, ky, kz, ry, rz)
    return (new[None], kept[None])


def solution(mesh):
    in_specs = (
        P("grp", "slab", None, None),
        P("grp", "slab", None, None),
        P(None, "slab", "grp", None),
        P("grp"),
    )
    out_specs = (P("grp", "slab", None, None), P("grp", "slab", None, None))
    return jax.shard_map(shards, mesh=mesh, in_specs=in_specs, out_specs=out_specs, check_vma=False)
```

```python
import functools

import jax
import jax.numpy as jnp
import numpy as np
from jax import lax
from jax.experimental import pallas as pl
from jax.experimental.pallas import tpu as pltpu
from jax.sharding import PartitionSpec as P

BLK = 32
ALPHA = 4.0 / 9.0
BETA = 1.0 / 36.0
COEF_A = 40.0 / 27.0
COEF_B = 25.0 / 54.0
RK_A = -5.0 / 9.0
RK_B = 15.0 / 16.0
STEP = 0.2
EVEN = (-0.0390625, 0.2734375, 0.8203125, -0.0546875)
ODD = (-0.0546875, 0.8203125, 0.2734375, -0.0390625)
MXU = 256


def band(count):
    eye = lambda k: np.eye(count, k=k)
    return eye(0) + ALPHA * (eye(1) + eye(-1)) + BETA * (eye(2) + eye(-2))


def blocked_operator(count, block):
    rhs = np.zeros((count, count))
    for i in range(count):
        for shift, coef in ((1, COEF_A / 2), (-1, -COEF_A / 2), (2, COEF_B / 4), (-2, -COEF_B / 4)):
            rhs[i, (i + shift) % count] += coef
    return np.kron(np.eye(count // block), np.linalg.inv(band(block))) @ rhs


def refine_operator(count):
    out = np.zeros((2 * count, count))
    for k in range(count):
        for t in range(4):
            out[2 * k, (k - 2 + t) % count] += EVEN[t]
            out[2 * k + 1, (k - 1 + t) % count] += ODD[t]
    return out


def split(x):
    hi = x.astype(jnp.bfloat16)
    return hi, (x - hi.astype(jnp.float32)).astype(jnp.bfloat16)


def host_split(x):
    x = jnp.asarray(np.asarray(x, np.float32))
    return jnp.stack(split(x))


def dot(a, b):
    return jnp.dot(a, b, preferred_element_type=jnp.float32)


def dot3(a, b):
    return dot(a[0], b[0]) + (dot(a[0], b[1]) + dot(a[1], b[0]))


def banded_lu(count):
    m = band(count)
    for k in range(count):
        for i in range(k + 1, min(k + 3, count)):
            m[i, k] /= m[k, k]
            m[i, k + 1 : min(k + 3, count)] -= m[i, k] * m[k, k + 1 : min(k + 3, count)]
    return m


def x_derivative(get, put, work, planes):
    m = banded_lu(planes)
    ratio = (COEF_B / 4) / (COEF_A / 2)
    y1 = y2 = None
    for i in range(planes):
        y = (get(i + 1) - get(i - 1)) + ratio * (get(i + 2) - get(i - 2))
        if i >= 1:
            y = y - float(m[i, i - 1]) * y1
        if i >= 2:
            y = y - float(m[i, i - 2]) * y2
        work[i] = y
        y1, y2 = y, y1
    x1 = x2 = None
    for i in reversed(range(planes)):
        inv = 1.0 / m[i, i]
        x = work[i] * float(inv * COEF_A / 2)
        if i + 1 < planes:
            x = x - float(m[i, i + 1] * inv) * x1
        if i + 2 < planes:
            x = x - float(m[i, i + 2] * inv) * x2
        put(i, x)
        x1, x2 = x, x1


SLOTS = ((0, 0), (0, 1), (0, 2), (1, 0), (1, 1), (2, 0), (2, 1))
FIRST, COUNT = (0, 3, 5), (3, 2, 2)


def pack_kernel(theta, velocity, head, tail, low, high, vel, sems):
    planes, ny, nz = theta.shape[1:]
    coarse, rows, nzc = velocity.shape[1:]
    copies = (
        pltpu.make_async_copy(theta.at[0, pl.ds(0, 2)], low, sems.at[0]),
        pltpu.make_async_copy(theta.at[0, pl.ds(planes - 2, 2)], high, sems.at[1]),
        pltpu.make_async_copy(velocity, vel, sems.at[2]),
    )
    for copy in copies:
        copy.start()
    for copy in copies:
        copy.wait()
    for out, edge, upper in ((head, low, False), (tail, high, True)):
        out[: 2 * ny] = edge[...].reshape(2 * ny, nz).astype(jnp.bfloat16)
        for q in range(8):
            c, k = SLOTS[min(q, 6)]
            k = coarse - COUNT[c] + k if upper else k
            top = 2 * ny + rows * (q // 2)
            out[top : top + rows, nzc * (q % 2) : nzc * (q % 2 + 1)] = vel[c, k]


def padded(th, tl, tr):
    planes, ny = th.shape[:2]

    def get(p):
        if p < 0:
            return tl[ny * (p + 2) : ny * (p + 3)].astype(jnp.float32)
        if p >= planes:
            return tr[ny * (p - planes) : ny * (p - planes + 1)].astype(jnp.float32)
        return th[p]

    return get


def first_kernel(kap, th, tl, tr, gx, halo, tail, head, kv, work):
    planes, ny, nz = th.shape
    kappa = kap[0]
    kv[...] = jnp.full(kv.shape, kappa, jnp.float32)

    def put(i, value):
        value = kappa * value
        gx[i] = value
        if i < 2:
            head[i] = value.astype(jnp.bfloat16)
        if i >= planes - 2:
            tail[i - (planes - 2)] = value.astype(jnp.bfloat16)

    halo[0] = tl[2 * ny :]
    halo[1] = tr[2 * ny :]
    x_derivative(padded(th, tl, tr), put, work, planes)


def flow_of(part, vel, halo, ry, rz):
    ngrp = len(vel)
    coarse, rows, nzc = vel[0].shape[1:]

    wide = ry[part[0]]

    def plane(c, k):
        if 0 <= k < coarse:
            got = [vel[g][c, k] for g in range(ngrp)]
        else:
            q = FIRST[c] + (COUNT[c] + k if k < 0 else k - coarse)
            top = rows * (q // 2)
            side = 0 if k < 0 else 1
            got = [halo[g][side, top : top + rows, nzc * (q % 2) : nzc * (q % 2 + 1)] for g in range(ngrp)]
        return jnp.concatenate([v.astype(jnp.float32) for v in got], axis=0)

    def fine(c, p):
        k = p // 2
        coefs, start = (EVEN, k - 2) if p % 2 == 0 else (ODD, k - 1)
        total = coefs[0] * plane(c, start)
        for t in range(1, 4):
            total = total + coefs[t] * plane(c, start + t)
        return total

    def flow(c, which):
        x = split(jnp.concatenate([fine(c, p) for p in which], axis=0))
        z = split(dot(x[0], rz[...]) + dot(x[1], rz[...]))
        return dot(wide, z[0]) + dot(wide, z[1])

    return flow


def is_inner(g, per, planes):
    return g * per >= 4 and (g + 1) * per <= planes - 4


def cross(flow, th, ky, kz, g, per):
    ny, nz = th.shape[1:]
    which = range(g * per, (g + 1) * per)
    x = th[g * per : (g + 1) * per].reshape(per * ny, nz)
    fy = split(flow(1, which) * x)
    fz = split(flow(2, which) * x)
    return (dot3(ky, fy) + dot3(fz, kz)).reshape(per, ny, nz)


def inner_kernel(ngrp, part, kv, th, gx, *refs):
    vel, (ky, kz, ky2, kz2, ry, rz, acc, flux) = refs[:ngrp], refs[ngrp:]
    planes, ny, nz = th.shape
    per = ky.shape[1] // ny
    kappa = kv[0:1, 0:1]
    flow = flow_of(part, vel, None, ry, rz)
    for g in range(planes // per):
        at = slice(g * per, (g + 1) * per)
        x = split(th[at].reshape(per * ny, nz))
        value = (-kappa * (dot3(ky2, x) + dot3(x, kz2))).reshape(per, ny, nz)
        if is_inner(g, per, planes):
            value = value + cross(flow, th, ky, kz, g, per)
            flux[at] = flow(0, range(g * per, (g + 1) * per)).reshape(per, ny, nz) * th[at] - gx[at]
        acc[at] = value


def final_kernel(ngrp, index, th, reg, part, inner, gx, tl, tr, gl, gr, *refs):
    vel, halo, (ky, kz, ry, rz, new, saved, flux, acc) = refs[:ngrp], refs[ngrp : 2 * ngrp], refs[2 * ngrp :]
    planes, ny, nz = th.shape
    per = ky.shape[1] // ny
    flow = flow_of(index, vel, halo, ry, rz)
    get = padded(th, tl, tr)
    outer = [g for g in range(planes // per) if not is_inner(g, per, planes)]
    for g in outer:
        acc[g * per : (g + 1) * per] = cross(flow, th, ky, kz, g, per) + part[g * per : (g + 1) * per]
    todo = [p for p in range(-2, planes + 2) if not is_inner(p // per, per, planes)]
    for start in range(0, len(todo), per):
        which = todo[start : start + per]
        f = flow(0, which + which[:1] * (per - len(which))).reshape(per, ny, nz)
        for i, p in enumerate(which):
            if p < 0:
                d = gl[p + 2].astype(jnp.float32)
            elif p >= planes:
                d = gr[p - planes].astype(jnp.float32)
            else:
                d = gx[p]
            flux[p + 2] = f[i] * get(p) - d

    def flux_at(p):
        return inner[p] if is_inner(p // per, per, planes) else flux[p + 2]

    def put(i, value):
        rest = part[i] if is_inner(i // per, per, planes) else acc[i]
        kept = RK_A * reg[i] - STEP * (value + rest)
        saved[i] = kept
        new[i] = th[i] + RK_B * kept

    x_derivative(flux_at, put, saved, planes)


def shards(theta, register, velocity, diffusivity):
    planes, ny, nz = theta.shape[1:]
    nslab, ngrp = lax.axis_size("slab"), lax.axis_size("grp")
    nyc, nzc = ny // 2, nz // 2
    per = max(1, MXU // ny)
    f32, bf16 = jnp.float32, jnp.bfloat16
    up = [(i, (i + 1) % nslab) for i in range(nslab)]
    down = [((i + 1) % nslab, i) for i in range(nslab)]
    op_y, op_z = blocked_operator(ny, BLK), blocked_operator(nz, BLK)
    eye = np.eye(per)
    ky2, kz2 = host_split(np.kron(eye, op_y @ op_y)), host_split((op_z @ op_z).T)
    ky, kz = host_split(np.kron(eye, op_y)), host_split(op_z.T)
    turned = [np.roll(refine_operator(nyc), -g * (nyc // ngrp), axis=1) for g in range(ngrp)]
    ry = jnp.asarray(np.stack([np.kron(eye, m) for m in turned]), bf16)
    rz = jnp.asarray(refine_operator(nzc).T, bf16)

    field, saved = theta[0], register[0]
    rows, coarse = velocity.shape[2], planes // 2
    full = jax.ShapeDtypeStruct((planes, ny, nz), f32)
    edge = jax.ShapeDtypeStruct((2, ny, nz), bf16)
    packed = jax.ShapeDtypeStruct((2 * ny + 4 * rows, nz), bf16)
    vmem = pl.BlockSpec(memory_space=pltpu.VMEM)
    smem = pl.BlockSpec(memory_space=pltpu.SMEM)
    params = pltpu.CompilerParams(vmem_limit_bytes=30 * 1024 * 1024)

    anywhere = pl.BlockSpec(memory_space=pl.ANY)
    head, tail = pl.pallas_call(
        pack_kernel,
        out_shape=(packed, packed),
        in_specs=[anywhere] * 2,
        out_specs=(vmem,) * 2,
        scratch_shapes=[
            pltpu.VMEM((2, ny, nz), f32),
            pltpu.VMEM((2, ny, nz), f32),
            pltpu.VMEM(velocity.shape, bf16),
            pltpu.SemaphoreType.DMA((3,)),
        ],
        name="pack",
    )(theta, velocity)

    def gathered(x):
        turns = [[((i + t) % ngrp, i) for i in range(ngrp)] for t in range(1, ngrp)]
        return [x] + [lax.ppermute(x, "grp", turn) for turn in turns]

    part = lax.axis_index("grp").astype(jnp.int32)[None]
    left = lax.ppermute(tail, "slab", up)
    right = lax.ppermute(head, "slab", down)
    vel = gathered(velocity)
    gx, halo, tail, head, kv = pl.pallas_call(
        first_kernel,
        out_shape=(full, jax.ShapeDtypeStruct((2, 4 * rows, nz), bf16), edge, edge, jax.ShapeDtypeStruct((8, 128), f32)),
        in_specs=[smem] + [vmem] * 3,
        out_specs=(vmem,) * 5,
        scratch_shapes=[pltpu.VMEM((planes, ny, nz), f32)],
        compiler_params=params,
        name="first",
    )(diffusivity, field, left, right)
    grad_l = lax.ppermute(tail, "slab", up)
    grad_r = lax.ppermute(head, "slab", down)
    halo = gathered(halo)
    acc, inner = pl.pallas_call(
        functools.partial(inner_kernel, ngrp),
        out_shape=(full, full),
        in_specs=[smem] + [vmem] * (9 + ngrp),
        out_specs=(vmem,) * 2,
        compiler_params=params,
        name="inner",
    )(part, kv, field, gx, *vel, ky, kz, ky2, kz2, ry, rz)
    new, kept = pl.pallas_call(
        functools.partial(final_kernel, ngrp),
        out_shape=(full, full),
        in_specs=[smem] + [vmem] * (13 + 2 * ngrp),
        out_specs=(vmem,) * 2,
        scratch_shapes=[pltpu.VMEM((planes + 4, ny, nz), f32), pltpu.VMEM((planes, ny, nz), f32)],
        compiler_params=params,
        name="final",
    )(part, field, saved, acc, inner, gx, left, right, grad_l, grad_r, *vel, *halo, ky, kz, ry, rz)
    return (new[None], kept[None])


def solution(mesh):
    in_specs = (
        P("grp", "slab", None, None),
        P("grp", "slab", None, None),
        P(None, "slab", "grp", None),
        P("grp"),
    )
    out_specs = (P("grp", "slab", None, None), P("grp", "slab", None, None))
    return jax.shard_map(shards, mesh=mesh, in_specs=in_specs, out_specs=out_specs, check_vma=False)
```

```python
import functools

import jax
import jax.numpy as jnp
import numpy as np
from jax import lax
from jax.experimental import pallas as pl
from jax.experimental.pallas import tpu as pltpu
from jax.sharding import PartitionSpec as P

BLK = 32
ALPHA = 4.0 / 9.0
BETA = 1.0 / 36.0
COEF_A = 40.0 / 27.0
COEF_B = 25.0 / 54.0
RK_A = -5.0 / 9.0
RK_B = 15.0 / 16.0
STEP = 0.2
EVEN = (-0.0390625, 0.2734375, 0.8203125, -0.0546875)
ODD = (-0.0546875, 0.8203125, 0.2734375, -0.0390625)
MXU = 256


def band(count):
    eye = lambda k: np.eye(count, k=k)
    return eye(0) + ALPHA * (eye(1) + eye(-1)) + BETA * (eye(2) + eye(-2))


def blocked_operator(count, block):
    rhs = np.zeros((count, count))
    for i in range(count):
        for shift, coef in ((1, COEF_A / 2), (-1, -COEF_A / 2), (2, COEF_B / 4), (-2, -COEF_B / 4)):
            rhs[i, (i + shift) % count] += coef
    return np.kron(np.eye(count // block), np.linalg.inv(band(block))) @ rhs


def refine_operator(count):
    out = np.zeros((2 * count, count))
    for k in range(count):
        for t in range(4):
            out[2 * k, (k - 2 + t) % count] += EVEN[t]
            out[2 * k + 1, (k - 1 + t) % count] += ODD[t]
    return out


def split(x):
    hi = x.astype(jnp.bfloat16)
    return hi, (x - hi.astype(jnp.float32)).astype(jnp.bfloat16)


def host_split(x):
    x = jnp.asarray(np.asarray(x, np.float32))
    return jnp.stack(split(x))


def host_stack(x):
    hi, lo = host_split(x)
    return jnp.concatenate([hi, lo, hi], axis=1)


def dot(a, b):
    return jnp.dot(a, b, preferred_element_type=jnp.float32)


def dot3(a, b):
    return dot(a[0], b[0]) + (dot(a[0], b[1]) + dot(a[1], b[0]))


def along_y(op, x, ny):
    out = []
    for top in range(0, x[0].shape[0], ny):
        hi, lo = x[0][top : top + ny], x[1][top : top + ny]
        out.append(dot(op[...], jnp.concatenate([hi, hi, lo], axis=0)))
    return jnp.concatenate(out, axis=0)


def banded_lu(count):
    m = band(count)
    for k in range(count):
        for i in range(k + 1, min(k + 3, count)):
            m[i, k] /= m[k, k]
            m[i, k + 1 : min(k + 3, count)] -= m[i, k] * m[k, k + 1 : min(k + 3, count)]
    return m


def x_derivative(get, put, work, planes):
    m = banded_lu(planes)
    ratio = (COEF_B / 4) / (COEF_A / 2)
    y1 = y2 = None
    for i in range(planes):
        y = (get(i + 1) - get(i - 1)) + ratio * (get(i + 2) - get(i - 2))
        if i >= 1:
            y = y - float(m[i, i - 1]) * y1
        if i >= 2:
            y = y - float(m[i, i - 2]) * y2
        work[i] = y
        y1, y2 = y, y1
    x1 = x2 = None
    for i in reversed(range(planes)):
        inv = 1.0 / m[i, i]
        x = work[i] * float(inv * COEF_A / 2)
        if i + 1 < planes:
            x = x - float(m[i, i + 1] * inv) * x1
        if i + 2 < planes:
            x = x - float(m[i, i + 2] * inv) * x2
        put(i, x)
        x1, x2 = x, x1


SLOTS = ((0, 0), (0, 1), (0, 2), (1, 0), (1, 1), (2, 0), (2, 1))
FIRST, COUNT = (0, 3, 5), (3, 2, 2)


def pack_kernel(theta, velocity, head, tail, low, high, vel, sems):
    planes, ny, nz = theta.shape[1:]
    coarse, rows, nzc = velocity.shape[1:]
    copies = (
        pltpu.make_async_copy(theta.at[0, pl.ds(0, 2)], low, sems.at[0]),
        pltpu.make_async_copy(theta.at[0, pl.ds(planes - 2, 2)], high, sems.at[1]),
        pltpu.make_async_copy(velocity, vel, sems.at[2]),
    )
    for copy in copies:
        copy.start()
    for copy in copies:
        copy.wait()
    for out, edge, upper in ((head, low, False), (tail, high, True)):
        out[: 2 * ny] = edge[...].reshape(2 * ny, nz).astype(jnp.bfloat16)
        for q in range(8):
            c, k = SLOTS[min(q, 6)]
            k = coarse - COUNT[c] + k if upper else k
            top = 2 * ny + rows * (q // 2)
            out[top : top + rows, nzc * (q % 2) : nzc * (q % 2 + 1)] = vel[c, k]


def padded(th, tl, tr):
    planes, ny = th.shape[:2]

    def get(p):
        if p < 0:
            return tl[ny * (p + 2) : ny * (p + 3)].astype(jnp.float32)
        if p >= planes:
            return tr[ny * (p - planes) : ny * (p - planes + 1)].astype(jnp.float32)
        return th[p]

    return get


def first_kernel(kap, th, tl, tr, gx, halo, tail, head, work):
    planes, ny, nz = th.shape
    kappa = kap[0]
    def put(i, value):
        value = kappa * value
        gx[i] = value
        if i < 2:
            head[i] = value.astype(jnp.bfloat16)
        if i >= planes - 2:
            tail[i - (planes - 2)] = value.astype(jnp.bfloat16)

    halo[0] = tl[2 * ny :]
    halo[1] = tr[2 * ny :]
    x_derivative(padded(th, tl, tr), put, work, planes)


def flow_of(part, vel, halo, ry, rz):
    ngrp = len(vel)
    coarse, rows, nzc = vel[0].shape[1:]

    wide = ry[part[0]]
    deep = jnp.concatenate([rz[...], rz[...]], axis=0)
    nyc = rows * ngrp

    def plane(c, k):
        if 0 <= k < coarse:
            got = [vel[g][c, k] for g in range(ngrp)]
        else:
            q = FIRST[c] + (COUNT[c] + k if k < 0 else k - coarse)
            top = rows * (q // 2)
            side = 0 if k < 0 else 1
            got = [halo[g][side, top : top + rows, nzc * (q % 2) : nzc * (q % 2 + 1)] for g in range(ngrp)]
        return jnp.concatenate([v.astype(jnp.float32) for v in got], axis=0)

    def fine(c, p):
        k = p // 2
        coefs, start = (EVEN, k - 2) if p % 2 == 0 else (ODD, k - 1)
        total = coefs[0] * plane(c, start)
        for t in range(1, 4):
            total = total + coefs[t] * plane(c, start + t)
        return total

    def flow(c, which):
        x = split(jnp.concatenate([fine(c, p) for p in which], axis=0))
        z = split(dot(jnp.concatenate(x, axis=1), deep))
        tops = range(0, z[0].shape[0], nyc)
        pairs = [jnp.concatenate([h[t : t + nyc] for h in z], axis=0) for t in tops]
        return jnp.concatenate([dot(wide, pair) for pair in pairs], axis=0)

    return flow


def is_inner(g, per, planes):
    return g * per >= 4 and (g + 1) * per <= planes - 4


def cross(flow, th, ky, kz, g, per):
    ny, nz = th.shape[1:]
    which = range(g * per, (g + 1) * per)
    x = th[g * per : (g + 1) * per].reshape(per * ny, nz)
    fy = split(flow(1, which) * x)
    fz = split(flow(2, which) * x)
    return (along_y(ky, fy, ny) + dot3(fz, kz)).reshape(per, ny, nz)


def inner_kernel(ngrp, part, kap, th, gx, *refs):
    vel, (ky, kz, ky2, kz2, ry, rz, acc, flux) = refs[:ngrp], refs[ngrp:]
    planes, ny, nz = th.shape
    per = max(1, MXU // ny)
    kappa = kap[0]
    flow = flow_of(part, vel, None, ry, rz)
    for g in range(planes // per):
        at = slice(g * per, (g + 1) * per)
        x = split(th[at].reshape(per * ny, nz))
        value = (-kappa * (along_y(ky2, x, ny) + dot3(x, kz2))).reshape(per, ny, nz)
        if is_inner(g, per, planes):
            value = value + cross(flow, th, ky, kz, g, per)
            flux[at] = flow(0, range(g * per, (g + 1) * per)).reshape(per, ny, nz) * th[at] - gx[at]
        acc[at] = value


def final_kernel(ngrp, index, th, reg, part, inner, gx, tl, tr, gl, gr, *refs):
    vel, halo, (ky, kz, ry, rz, new, saved, flux, acc) = refs[:ngrp], refs[ngrp : 2 * ngrp], refs[2 * ngrp :]
    planes, ny, nz = th.shape
    per = max(1, MXU // ny)
    flow = flow_of(index, vel, halo, ry, rz)
    get = padded(th, tl, tr)
    outer = [g for g in range(planes // per) if not is_inner(g, per, planes)]
    for g in outer:
        acc[g * per : (g + 1) * per] = cross(flow, th, ky, kz, g, per) + part[g * per : (g + 1) * per]
    todo = [p for p in range(-2, planes + 2) if not is_inner(p // per, per, planes)]
    for start in range(0, len(todo), per):
        which = todo[start : start + per]
        f = flow(0, which + which[:1] * (per - len(which))).reshape(per, ny, nz)
        for i, p in enumerate(which):
            if p < 0:
                d = gl[p + 2].astype(jnp.float32)
            elif p >= planes:
                d = gr[p - planes].astype(jnp.float32)
            else:
                d = gx[p]
            flux[p + 2] = f[i] * get(p) - d

    def flux_at(p):
        return inner[p] if is_inner(p // per, per, planes) else flux[p + 2]

    def put(i, value):
        rest = part[i] if is_inner(i // per, per, planes) else acc[i]
        kept = RK_A * reg[i] - STEP * (value + rest)
        saved[i] = kept
        new[i] = th[i] + RK_B * kept

    x_derivative(flux_at, put, saved, planes)


def shards(theta, register, velocity, diffusivity):
    planes, ny, nz = theta.shape[1:]
    nslab, ngrp = lax.axis_size("slab"), lax.axis_size("grp")
    nyc, nzc = ny // 2, nz // 2
    f32, bf16 = jnp.float32, jnp.bfloat16
    up = [(i, (i + 1) % nslab) for i in range(nslab)]
    down = [((i + 1) % nslab, i) for i in range(nslab)]
    op_y, op_z = blocked_operator(ny, BLK), blocked_operator(nz, BLK)
    ky2, kz2 = host_stack(op_y @ op_y), host_split((op_z @ op_z).T)
    ky, kz = host_stack(op_y), host_split(op_z.T)
    turned = [np.roll(refine_operator(nyc), -g * (nyc // ngrp), axis=1) for g in range(ngrp)]
    ry = jnp.asarray(np.stack([np.tile(m, (1, 2)) for m in turned]), bf16)
    rz = jnp.asarray(refine_operator(nzc).T, bf16)

    field, saved = theta[0], register[0]
    rows, coarse = velocity.shape[2], planes // 2
    full = jax.ShapeDtypeStruct((planes, ny, nz), f32)
    edge = jax.ShapeDtypeStruct((2, ny, nz), bf16)
    packed = jax.ShapeDtypeStruct((2 * ny + 4 * rows, nz), bf16)
    vmem = pl.BlockSpec(memory_space=pltpu.VMEM)
    smem = pl.BlockSpec(memory_space=pltpu.SMEM)
    grant = lambda mib: pltpu.CompilerParams(vmem_limit_bytes=mib * 1024 * 1024)

    anywhere = pl.BlockSpec(memory_space=pl.ANY)
    head, tail = pl.pallas_call(
        pack_kernel,
        out_shape=(packed, packed),
        in_specs=[anywhere] * 2,
        out_specs=(vmem,) * 2,
        scratch_shapes=[
            pltpu.VMEM((2, ny, nz), f32),
            pltpu.VMEM((2, ny, nz), f32),
            pltpu.VMEM(velocity.shape, bf16),
            pltpu.SemaphoreType.DMA((3,)),
        ],
        compiler_params=grant(4),
        name="pack",
    )(theta, velocity)

    def gathered(x):
        turns = [[((i + t) % ngrp, i) for i in range(ngrp)] for t in range(1, ngrp)]
        return [x] + [lax.ppermute(x, "grp", turn) for turn in turns]

    part = lax.axis_index("grp").astype(jnp.int32)[None]
    left = lax.ppermute(tail, "slab", up)
    right = lax.ppermute(head, "slab", down)
    vel = gathered(velocity)
    gx, halo, tail, head = pl.pallas_call(
        first_kernel,
        out_shape=(full, jax.ShapeDtypeStruct((2, 4 * rows, nz), bf16), edge, edge),
        in_specs=[smem] + [vmem] * 3,
        out_specs=(vmem,) * 4,
        scratch_shapes=[pltpu.VMEM((planes, ny, nz), f32)],
        compiler_params=grant(8),
        name="first",
    )(diffusivity, field, left, right)
    grad_l = lax.ppermute(tail, "slab", up)
    grad_r = lax.ppermute(head, "slab", down)
    halo = gathered(halo)
    acc, inner = pl.pallas_call(
        functools.partial(inner_kernel, ngrp),
        out_shape=(full, full),
        in_specs=[smem] * 2 + [vmem] * (8 + ngrp),
        out_specs=(vmem,) * 2,
        compiler_params=grant(14),
        name="inner",
    )(part, diffusivity, field, gx, *vel, ky, kz, ky2, kz2, ry, rz)
    new, kept = pl.pallas_call(
        functools.partial(final_kernel, ngrp),
        out_shape=(full, full),
        in_specs=[smem] + [vmem] * (13 + 2 * ngrp),
        out_specs=(vmem,) * 2,
        scratch_shapes=[pltpu.VMEM((planes + 4, ny, nz), f32), pltpu.VMEM((planes, ny, nz), f32)],
        compiler_params=grant(14),
        name="final",
    )(part, field, saved, acc, inner, gx, left, right, grad_l, grad_r, *vel, *halo, ky, kz, ry, rz)
    return (new[None], kept[None])


def solution(mesh):
    in_specs = (
        P("grp", "slab", None, None),
        P("grp", "slab", None, None),
        P(None, "slab", "grp", None),
        P("grp"),
    )
    out_specs = (P("grp", "slab", None, None), P("grp", "slab", None, None))
    return jax.shard_map(shards, mesh=mesh, in_specs=in_specs, out_specs=out_specs, check_vma=False)
```

```python
import functools

import jax
import jax.numpy as jnp
import numpy as np
from jax import lax
from jax.experimental import pallas as pl
from jax.experimental.pallas import tpu as pltpu
from jax.sharding import PartitionSpec as P

BLK = 32
ALPHA = 4.0 / 9.0
BETA = 1.0 / 36.0
COEF_A = 40.0 / 27.0
COEF_B = 25.0 / 54.0
RK_A = -5.0 / 9.0
RK_B = 15.0 / 16.0
STEP = 0.2
EVEN = (-0.0390625, 0.2734375, 0.8203125, -0.0546875)
ODD = (-0.0546875, 0.8203125, 0.2734375, -0.0390625)
MXU = 256


def band(count):
    eye = lambda k: np.eye(count, k=k)
    return eye(0) + ALPHA * (eye(1) + eye(-1)) + BETA * (eye(2) + eye(-2))


def blocked_operator(count, block):
    rhs = np.zeros((count, count))
    for i in range(count):
        for shift, coef in ((1, COEF_A / 2), (-1, -COEF_A / 2), (2, COEF_B / 4), (-2, -COEF_B / 4)):
            rhs[i, (i + shift) % count] += coef
    return np.kron(np.eye(count // block), np.linalg.inv(band(block))) @ rhs


def refine_operator(count):
    out = np.zeros((2 * count, count))
    for k in range(count):
        for t in range(4):
            out[2 * k, (k - 2 + t) % count] += EVEN[t]
            out[2 * k + 1, (k - 1 + t) % count] += ODD[t]
    return out


def split(x):
    hi = x.astype(jnp.bfloat16)
    return hi, (x - hi.astype(jnp.float32)).astype(jnp.bfloat16)


def host_split(x):
    x = jnp.asarray(np.asarray(x, np.float32))
    return jnp.stack(split(x))


def host_stack(x):
    hi, lo = host_split(x)
    return jnp.concatenate([hi, lo, hi], axis=1)


def dot(a, b):
    return jnp.dot(a, b, preferred_element_type=jnp.float32)


def dot3(a, b):
    return dot(a[0], b[0]) + (dot(a[0], b[1]) + dot(a[1], b[0]))


def widen(half):
    mid = half.shape[1] // 2
    return [jnp.concatenate([k, jnp.concatenate([k[mid:], k[:mid]], axis=0)], axis=1) for k in (half[0], half[1])]


def along_y(op, x, ny):
    out = []
    for top in range(0, x[0].shape[0], ny):
        hi, lo = x[0][top : top + ny], x[1][top : top + ny]
        out.append(dot(op[...], jnp.concatenate([hi, hi, lo], axis=0)))
    return jnp.concatenate(out, axis=0)


def banded_lu(count):
    m = band(count)
    for k in range(count):
        for i in range(k + 1, min(k + 3, count)):
            m[i, k] /= m[k, k]
            m[i, k + 1 : min(k + 3, count)] -= m[i, k] * m[k, k + 1 : min(k + 3, count)]
    return m


def x_derivative(get, put, work, planes):
    m = banded_lu(planes)
    ratio = (COEF_B / 4) / (COEF_A / 2)
    y1 = y2 = None
    for i in range(planes):
        y = (get(i + 1) - get(i - 1)) + ratio * (get(i + 2) - get(i - 2))
        if i >= 1:
            y = y - float(m[i, i - 1]) * y1
        if i >= 2:
            y = y - float(m[i, i - 2]) * y2
        work[i] = y
        y1, y2 = y, y1
    x1 = x2 = None
    for i in reversed(range(planes)):
        inv = 1.0 / m[i, i]
        x = work[i] * float(inv * COEF_A / 2)
        if i + 1 < planes:
            x = x - float(m[i, i + 1] * inv) * x1
        if i + 2 < planes:
            x = x - float(m[i, i + 2] * inv) * x2
        put(i, x)
        x1, x2 = x, x1


SLOTS = ((0, 0), (0, 1), (0, 2), (1, 0), (1, 1), (2, 0), (2, 1))
FIRST, COUNT = (0, 3, 5), (3, 2, 2)


def pack_kernel(theta, velocity, head, tail, vel, low, high, sems):
    planes, ny, nz = theta.shape[1:]
    coarse, rows, nzc = velocity.shape[1:]
    copies = (
        pltpu.make_async_copy(theta.at[0, pl.ds(0, 2)], low, sems.at[0]),
        pltpu.make_async_copy(theta.at[0, pl.ds(planes - 2, 2)], high, sems.at[1]),
        pltpu.make_async_copy(velocity, vel, sems.at[2]),
    )
    for copy in copies:
        copy.start()
    for copy in copies:
        copy.wait()
    for out, edge, upper in ((head, low, False), (tail, high, True)):
        out[: 2 * ny] = edge[...].reshape(2 * ny, nz).astype(jnp.bfloat16)
        for q in range(8):
            c, k = SLOTS[min(q, 6)]
            k = coarse - COUNT[c] + k if upper else k
            top = 2 * ny + rows * (q // 2)
            out[top : top + rows, nzc * (q % 2) : nzc * (q % 2 + 1)] = vel[c, k]


def padded(th, tl, tr):
    planes, ny = th.shape[:2]

    def get(p):
        if p < 0:
            return tl[ny * (p + 2) : ny * (p + 3)].astype(jnp.float32)
        if p >= planes:
            return tr[ny * (p - planes) : ny * (p - planes + 1)].astype(jnp.float32)
        return th[p]

    return get


def first_kernel(kap, th, tl, tr, gx, halo, tail, head, work):
    planes, ny, nz = th.shape
    kappa = kap[0]
    def put(i, value):
        value = kappa * value
        gx[i] = value
        if i < 2:
            head[i] = value.astype(jnp.bfloat16)
        if i >= planes - 2:
            tail[i - (planes - 2)] = value.astype(jnp.bfloat16)

    halo[0] = tl[2 * ny :]
    halo[1] = tr[2 * ny :]
    x_derivative(padded(th, tl, tr), put, work, planes)


def flow_of(part, vel, halo, ry, rz):
    ngrp = len(vel)
    coarse, rows, nzc = vel[0].shape[1:]

    wide = ry[part[0]]
    deep = jnp.concatenate([rz[...], rz[...]], axis=0)
    nyc = rows * ngrp

    def plane(c, k):
        if 0 <= k < coarse:
            got = [vel[g][c, k] for g in range(ngrp)]
        else:
            q = FIRST[c] + (COUNT[c] + k if k < 0 else k - coarse)
            top = rows * (q // 2)
            side = 0 if k < 0 else 1
            got = [halo[g][side, top : top + rows, nzc * (q % 2) : nzc * (q % 2 + 1)] for g in range(ngrp)]
        return jnp.concatenate([v.astype(jnp.float32) for v in got], axis=0)

    def fine(c, p):
        k = p // 2
        coefs, start = (EVEN, k - 2) if p % 2 == 0 else (ODD, k - 1)
        total = coefs[0] * plane(c, start)
        for t in range(1, 4):
            total = total + coefs[t] * plane(c, start + t)
        return total

    def flow(c, which):
        x = split(jnp.concatenate([fine(c, p) for p in which], axis=0))
        z = split(dot(jnp.concatenate(x, axis=1), deep))
        tops = range(0, z[0].shape[0], nyc)
        pairs = [jnp.concatenate([h[t : t + nyc] for h in z], axis=0) for t in tops]
        return jnp.concatenate([dot(wide, pair) for pair in pairs], axis=0)

    return flow


def is_inner(g, per, planes):
    return g * per >= 4 and (g + 1) * per <= planes - 4


def cross(flow, th, ky, kz, g, per):
    ny, nz = th.shape[1:]
    which = range(g * per, (g + 1) * per)
    x = th[g * per : (g + 1) * per].reshape(per * ny, nz)
    fy = split(flow(1, which) * x)
    fz = split(flow(2, which) * x)
    return (along_y(ky, fy, ny) + dot3(fz, kz)).reshape(per, ny, nz)


def inner_kernel(ngrp, part, kap, th, gx, *refs):
    vel, (ky, kz, ky2, kz2, ry, rz, acc, flux) = refs[:ngrp], refs[ngrp:]
    planes, ny, nz = th.shape
    per = max(1, MXU // ny)
    kappa = kap[0]
    kz, kz2 = widen(kz), widen(kz2)
    flow = flow_of(part, vel, None, ry, rz)
    for g in range(planes // per):
        at = slice(g * per, (g + 1) * per)
        x = split(th[at].reshape(per * ny, nz))
        value = (-kappa * (along_y(ky2, x, ny) + dot3(x, kz2))).reshape(per, ny, nz)
        if is_inner(g, per, planes):
            value = value + cross(flow, th, ky, kz, g, per)
            flux[at] = flow(0, range(g * per, (g + 1) * per)).reshape(per, ny, nz) * th[at] - gx[at]
        acc[at] = value


def final_kernel(ngrp, index, th, reg, part, inner, gx, tl, tr, gl, gr, *refs):
    vel, halo, (ky, kz, ry, rz, new_hbm, saved_hbm, new, saved, flux, acc, sems) = refs[:ngrp], refs[ngrp : 2 * ngrp], refs[2 * ngrp :]
    planes, ny, nz = th.shape
    per = max(1, MXU // ny)
    kz = widen(kz)
    flow = flow_of(index, vel, halo, ry, rz)
    get = padded(th, tl, tr)
    outer = [g for g in range(planes // per) if not is_inner(g, per, planes)]
    for g in outer:
        acc[g * per : (g + 1) * per] = cross(flow, th, ky, kz, g, per) + part[g * per : (g + 1) * per]
    todo = [p for p in range(-2, planes + 2) if not is_inner(p // per, per, planes)]
    for start in range(0, len(todo), per):
        which = todo[start : start + per]
        f = flow(0, which + which[:1] * (per - len(which))).reshape(per, ny, nz)
        for i, p in enumerate(which):
            if p < 0:
                d = gl[p + 2].astype(jnp.float32)
            elif p >= planes:
                d = gr[p - planes].astype(jnp.float32)
            else:
                d = gx[p]
            flux[p + 2] = f[i] * get(p) - d

    def flux_at(p):
        return inner[p] if is_inner(p // per, per, planes) else flux[p + 2]

    def put(i, value):
        rest = part[i] if is_inner(i // per, per, planes) else acc[i]
        kept = RK_A * reg[i] - STEP * (value + rest)
        saved[i] = kept
        new[i] = th[i] + RK_B * kept
        if i % per == 0:
            at = pl.ds(i, per)
            for k, (src, dst) in enumerate(((saved, saved_hbm), (new, new_hbm))):
                copies.append(pltpu.make_async_copy(src.at[at], dst.at[at], sems.at[2 * (i // per) + k]))
                copies[-1].start()

    copies = []
    x_derivative(flux_at, put, saved, planes)
    for copy in copies:
        copy.wait()


def shards(theta, register, velocity, diffusivity):
    planes, ny, nz = theta.shape[1:]
    nslab, ngrp = lax.axis_size("slab"), lax.axis_size("grp")
    nyc, nzc = ny // 2, nz // 2
    f32, bf16 = jnp.float32, jnp.bfloat16
    up = [(i, (i + 1) % nslab) for i in range(nslab)]
    down = [((i + 1) % nslab, i) for i in range(nslab)]
    op_y, op_z = blocked_operator(ny, BLK), blocked_operator(nz, BLK)
    ky2, kz2 = host_stack(op_y @ op_y), host_split((op_z @ op_z).T[:, : nz // 2])
    ky, kz = host_stack(op_y), host_split(op_z.T[:, : nz // 2])
    turned = [np.roll(refine_operator(nyc), -g * (nyc // ngrp), axis=1) for g in range(ngrp)]
    ry = jnp.asarray(np.stack([np.tile(m, (1, 2)) for m in turned]), bf16)
    rz = jnp.asarray(refine_operator(nzc).T, bf16)

    field, saved = theta[0], register[0]
    rows, coarse = velocity.shape[2], planes // 2
    full = jax.ShapeDtypeStruct((planes, ny, nz), f32)
    edge = jax.ShapeDtypeStruct((2, ny, nz), bf16)
    packed = jax.ShapeDtypeStruct((2 * ny + 4 * rows, nz), bf16)
    vmem = pl.BlockSpec(memory_space=pltpu.VMEM)
    smem = pl.BlockSpec(memory_space=pltpu.SMEM)
    grant = lambda mib: pltpu.CompilerParams(vmem_limit_bytes=mib * 1024 * 1024)

    head, tail, own = pl.pallas_call(
        pack_kernel,
        out_shape=(packed, packed, jax.ShapeDtypeStruct(velocity.shape, bf16)),
        in_specs=[pl.BlockSpec(memory_space=pltpu.HBM)] * 2,
        out_specs=(vmem,) * 3,
        scratch_shapes=[
            pltpu.VMEM((2, ny, nz), f32),
            pltpu.VMEM((2, ny, nz), f32),
            pltpu.SemaphoreType.DMA((3,)),
        ],
        compiler_params=grant(4),
        name="pack",
    )(theta, velocity)

    def gathered(x):
        turns = [[((i + t) % ngrp, i) for i in range(ngrp)] for t in range(1, ngrp)]
        return [x] + [lax.ppermute(x, "grp", turn) for turn in turns]

    part = lax.axis_index("grp").astype(jnp.int32)[None]
    left = lax.ppermute(tail, "slab", up)
    right = lax.ppermute(head, "slab", down)
    vel = gathered(own)
    gx, halo, tail, head = pl.pallas_call(
        first_kernel,
        out_shape=(full, jax.ShapeDtypeStruct((2, 4 * rows, nz), bf16), edge, edge),
        in_specs=[smem] + [vmem] * 3,
        out_specs=(vmem,) * 4,
        scratch_shapes=[pltpu.VMEM((planes, ny, nz), f32)],
        compiler_params=grant(8),
        name="first",
    )(diffusivity, field, left, right)
    grad_l = lax.ppermute(tail, "slab", up)
    grad_r = lax.ppermute(head, "slab", down)
    halo = gathered(halo)
    acc, inner = pl.pallas_call(
        functools.partial(inner_kernel, ngrp),
        out_shape=(full, full),
        in_specs=[smem] * 2 + [vmem] * (8 + ngrp),
        out_specs=(vmem,) * 2,
        compiler_params=grant(14),
        name="inner",
    )(part, diffusivity, field, gx, *vel, ky, kz, ky2, kz2, ry, rz)
    new, kept = pl.pallas_call(
        functools.partial(final_kernel, ngrp),
        out_shape=(full, full),
        in_specs=[smem] + [vmem] * (13 + 2 * ngrp),
        out_specs=(pl.BlockSpec(memory_space=pltpu.HBM),) * 2,
        scratch_shapes=[
            pltpu.VMEM((planes, ny, nz), f32),
            pltpu.VMEM((planes, ny, nz), f32),
            pltpu.VMEM((planes + 4, ny, nz), f32),
            pltpu.VMEM((planes, ny, nz), f32),
            pltpu.SemaphoreType.DMA((2 * planes,)),
        ],
        compiler_params=grant(14),
        name="final",
    )(part, field, saved, acc, inner, gx, left, right, grad_l, grad_r, *vel, *halo, ky, kz, ry, rz)
    return (new[None], kept[None])


def solution(mesh):
    in_specs = (
        P("grp", "slab", None, None),
        P("grp", "slab", None, None),
        P(None, "slab", "grp", None),
        P("grp"),
    )
    out_specs = (P("grp", "slab", None, None), P("grp", "slab", None, None))
    return jax.shard_map(shards, mesh=mesh, in_specs=in_specs, out_specs=out_specs, check_vma=False)
```

```python
import functools

import jax
import jax.numpy as jnp
import numpy as np
from jax import lax
from jax.experimental import pallas as pl
from jax.experimental.pallas import tpu as pltpu
from jax.sharding import PartitionSpec as P

BLK = 32
ALPHA = 4.0 / 9.0
BETA = 1.0 / 36.0
COEF_A = 40.0 / 27.0
COEF_B = 25.0 / 54.0
RK_A = -5.0 / 9.0
RK_B = 15.0 / 16.0
STEP = 0.2
EVEN = (-0.0390625, 0.2734375, 0.8203125, -0.0546875)
ODD = (-0.0546875, 0.8203125, 0.2734375, -0.0390625)
MXU = 256


def band(count):
    eye = lambda k: np.eye(count, k=k)
    return eye(0) + ALPHA * (eye(1) + eye(-1)) + BETA * (eye(2) + eye(-2))


def blocked_operator(count, block):
    rhs = np.zeros((count, count))
    for i in range(count):
        for shift, coef in ((1, COEF_A / 2), (-1, -COEF_A / 2), (2, COEF_B / 4), (-2, -COEF_B / 4)):
            rhs[i, (i + shift) % count] += coef
    return np.kron(np.eye(count // block), np.linalg.inv(band(block))) @ rhs


def refine_operator(count):
    out = np.zeros((2 * count, count))
    for k in range(count):
        for t in range(4):
            out[2 * k, (k - 2 + t) % count] += EVEN[t]
            out[2 * k + 1, (k - 1 + t) % count] += ODD[t]
    return out


def split(x):
    hi = x.astype(jnp.bfloat16)
    return hi, (x - hi.astype(jnp.float32)).astype(jnp.bfloat16)


def host_split(x):
    x = jnp.asarray(np.asarray(x, np.float32))
    return jnp.stack(split(x))


def host_stack(x):
    hi, lo = host_split(x)
    return jnp.concatenate([hi, lo, hi], axis=1)


def dot(a, b):
    return jnp.dot(a, b, preferred_element_type=jnp.float32)


def dot3(a, b):
    return dot(a[0], b[0]) + (dot(a[0], b[1]) + dot(a[1], b[0]))


def widen(half):
    mid = half.shape[1] // 2
    return [jnp.concatenate([k, jnp.concatenate([k[mid:], k[:mid]], axis=0)], axis=1) for k in (half[0], half[1])]


def along_y(op, x, ny):
    out = []
    for top in range(0, x[0].shape[0], ny):
        hi, lo = x[0][top : top + ny], x[1][top : top + ny]
        out.append(dot(op[...], jnp.concatenate([hi, hi, lo], axis=0)))
    return jnp.concatenate(out, axis=0)


def banded_lu(count):
    m = band(count)
    for k in range(count):
        for i in range(k + 1, min(k + 3, count)):
            m[i, k] /= m[k, k]
            m[i, k + 1 : min(k + 3, count)] -= m[i, k] * m[k, k + 1 : min(k + 3, count)]
    return m


def x_derivative(get, put, work, planes):
    m = banded_lu(planes)
    ratio = (COEF_B / 4) / (COEF_A / 2)
    y1 = y2 = None
    for i in range(planes):
        y = (get(i + 1) - get(i - 1)) + ratio * (get(i + 2) - get(i - 2))
        if i >= 1:
            y = y - float(m[i, i - 1]) * y1
        if i >= 2:
            y = y - float(m[i, i - 2]) * y2
        work[i] = y
        y1, y2 = y, y1
    x1 = x2 = None
    for i in reversed(range(planes)):
        inv = 1.0 / m[i, i]
        x = work[i] * float(inv * COEF_A / 2)
        if i + 1 < planes:
            x = x - float(m[i, i + 1] * inv) * x1
        if i + 2 < planes:
            x = x - float(m[i, i + 2] * inv) * x2
        put(i, x)
        x1, x2 = x, x1


SLOTS = ((0, 0), (0, 1), (0, 2), (1, 0), (1, 1), (2, 0), (2, 1))
FIRST, COUNT = (0, 3, 5), (3, 2, 2)


def pack_kernel(theta, velocity, head, tail, vel, low, high, sems):
    planes, ny, nz = theta.shape[1:]
    coarse, rows, nzc = velocity.shape[1:]
    copies = (
        pltpu.make_async_copy(theta.at[0, pl.ds(0, 2)], low, sems.at[0]),
        pltpu.make_async_copy(theta.at[0, pl.ds(planes - 2, 2)], high, sems.at[1]),
        pltpu.make_async_copy(velocity, vel, sems.at[2]),
    )
    for copy in copies:
        copy.start()
    for copy in copies:
        copy.wait()
    for out, edge, upper in ((head, low, False), (tail, high, True)):
        out[: 2 * ny] = edge[...].reshape(2 * ny, nz).astype(jnp.bfloat16)
        for q in range(8):
            c, k = SLOTS[min(q, 6)]
            k = coarse - COUNT[c] + k if upper else k
            top = 2 * ny + rows * (q // 2)
            out[top : top + rows, nzc * (q % 2) : nzc * (q % 2 + 1)] = vel[c, k]


def padded(th, tl, tr):
    planes, ny = th.shape[:2]

    def get(p):
        if p < 0:
            return tl[ny * (p + 2) : ny * (p + 3)].astype(jnp.float32)
        if p >= planes:
            return tr[ny * (p - planes) : ny * (p - planes + 1)].astype(jnp.float32)
        return th[p]

    return get


def first_kernel(kap, th, tl, tr, gx, halo, tail, head, work):
    planes, ny, nz = th.shape
    kappa = kap[0:1, 0:1]
    def put(i, value):
        value = kappa * value
        gx[i] = value
        if i < 2:
            head[i] = value.astype(jnp.bfloat16)
        if i >= planes - 2:
            tail[i - (planes - 2)] = value.astype(jnp.bfloat16)

    halo[0] = tl[2 * ny :]
    halo[1] = tr[2 * ny :]
    x_derivative(padded(th, tl, tr), put, work, planes)


def flow_of(part, vel, halo, ry, rz):
    ngrp = len(vel)
    coarse, rows, nzc = vel[0].shape[1:]

    wide = ry[part[0]]
    deep = jnp.concatenate([rz[...], rz[...]], axis=0)
    nyc = rows * ngrp

    def plane(c, k):
        if 0 <= k < coarse:
            got = [vel[g][c, k] for g in range(ngrp)]
        else:
            q = FIRST[c] + (COUNT[c] + k if k < 0 else k - coarse)
            top = rows * (q // 2)
            side = 0 if k < 0 else 1
            got = [halo[g][side, top : top + rows, nzc * (q % 2) : nzc * (q % 2 + 1)] for g in range(ngrp)]
        return jnp.concatenate([v.astype(jnp.float32) for v in got], axis=0)

    def fine(c, p):
        k = p // 2
        coefs, start = (EVEN, k - 2) if p % 2 == 0 else (ODD, k - 1)
        total = coefs[0] * plane(c, start)
        for t in range(1, 4):
            total = total + coefs[t] * plane(c, start + t)
        return total

    def flow(c, which):
        x = split(jnp.concatenate([fine(c, p) for p in which], axis=0))
        z = split(dot(jnp.concatenate(x, axis=1), deep))
        tops = range(0, z[0].shape[0], nyc)
        pairs = [jnp.concatenate([h[t : t + nyc] for h in z], axis=0) for t in tops]
        return jnp.concatenate([dot(wide, pair) for pair in pairs], axis=0)

    return flow


def is_inner(g, per, planes):
    return g * per >= 4 and (g + 1) * per <= planes - 4


def cross(flow, th, ky, kz, g, per):
    ny, nz = th.shape[1:]
    which = range(g * per, (g + 1) * per)
    x = th[g * per : (g + 1) * per].reshape(per * ny, nz)
    fy = split(flow(1, which) * x)
    fz = split(flow(2, which) * x)
    return (along_y(ky, fy, ny) + dot3(fz, kz)).reshape(per, ny, nz)


def inner_kernel(ngrp, part, kap, th, gx, *refs):
    vel, (ky, kz, ky2, kz2, ry, rz, acc, flux) = refs[:ngrp], refs[ngrp:]
    planes, ny, nz = th.shape
    per = max(1, MXU // ny)
    kappa = kap[0:1, 0:1]
    kz, kz2 = widen(kz), widen(kz2)
    flow = flow_of(part, vel, None, ry, rz)
    for g in range(planes // per):
        at = slice(g * per, (g + 1) * per)
        x = split(th[at].reshape(per * ny, nz))
        value = (-kappa * (along_y(ky2, x, ny) + dot3(x, kz2))).reshape(per, ny, nz)
        if is_inner(g, per, planes):
            value = value + cross(flow, th, ky, kz, g, per)
            flux[at] = flow(0, range(g * per, (g + 1) * per)).reshape(per, ny, nz) * th[at] - gx[at]
        acc[at] = value


def final_kernel(ngrp, index, th, reg, part, inner, gx, tl, tr, gl, gr, *refs):
    vel, halo, (ky, kz, ry, rz, new_hbm, saved_hbm, new, saved, flux, acc, sems) = refs[:ngrp], refs[ngrp : 2 * ngrp], refs[2 * ngrp :]
    planes, ny, nz = th.shape
    per = max(1, MXU // ny)
    kz = widen(kz)
    flow = flow_of(index, vel, halo, ry, rz)
    get = padded(th, tl, tr)
    outer = [g for g in range(planes // per) if not is_inner(g, per, planes)]
    for g in outer:
        acc[g * per : (g + 1) * per] = cross(flow, th, ky, kz, g, per) + part[g * per : (g + 1) * per]
    todo = [p for p in range(-2, planes + 2) if not is_inner(p // per, per, planes)]
    for start in range(0, len(todo), per):
        which = todo[start : start + per]
        f = flow(0, which + which[:1] * (per - len(which))).reshape(per, ny, nz)
        for i, p in enumerate(which):
            if p < 0:
                d = gl[p + 2].astype(jnp.float32)
            elif p >= planes:
                d = gr[p - planes].astype(jnp.float32)
            else:
                d = gx[p]
            flux[p + 2] = f[i] * get(p) - d

    def flux_at(p):
        return inner[p] if is_inner(p // per, per, planes) else flux[p + 2]

    def put(i, value):
        rest = part[i] if is_inner(i // per, per, planes) else acc[i]
        kept = RK_A * reg[i] - STEP * (value + rest)
        saved[i] = kept
        new[i] = th[i] + RK_B * kept
        if i % per == 0:
            at = pl.ds(i, per)
            for k, (src, dst) in enumerate(((saved, saved_hbm), (new, new_hbm))):
                copies.append(pltpu.make_async_copy(src.at[at], dst.at[at], sems.at[2 * (i // per) + k]))
                copies[-1].start()

    copies = []
    x_derivative(flux_at, put, saved, planes)
    for copy in copies:
        copy.wait()


def shards(theta, register, velocity, diffusivity):
    planes, ny, nz = theta.shape[1:]
    nslab, ngrp = lax.axis_size("slab"), lax.axis_size("grp")
    nyc, nzc = ny // 2, nz // 2
    f32, bf16 = jnp.float32, jnp.bfloat16
    up = [(i, (i + 1) % nslab) for i in range(nslab)]
    down = [((i + 1) % nslab, i) for i in range(nslab)]
    op_y, op_z = blocked_operator(ny, BLK), blocked_operator(nz, BLK)
    ky2, kz2 = host_stack(op_y @ op_y), host_split((op_z @ op_z).T[:, : nz // 2])
    ky, kz = host_stack(op_y), host_split(op_z.T[:, : nz // 2])
    turned = [np.roll(refine_operator(nyc), -g * (nyc // ngrp), axis=1) for g in range(ngrp)]
    ry = jnp.asarray(np.stack([np.tile(m, (1, 2)) for m in turned]), bf16)
    rz = jnp.asarray(refine_operator(nzc).T, bf16)

    field, saved = theta[0], register[0]
    rows, coarse = velocity.shape[2], planes // 2
    full = jax.ShapeDtypeStruct((planes, ny, nz), f32)
    edge = jax.ShapeDtypeStruct((2, ny, nz), bf16)
    packed = jax.ShapeDtypeStruct((2 * ny + 4 * rows, nz), bf16)
    vmem = pl.BlockSpec(memory_space=pltpu.VMEM)
    smem = pl.BlockSpec(memory_space=pltpu.SMEM)
    grant = lambda mib: pltpu.CompilerParams(vmem_limit_bytes=mib * 1024 * 1024)

    head, tail, own = pl.pallas_call(
        pack_kernel,
        out_shape=(packed, packed, jax.ShapeDtypeStruct(velocity.shape, bf16)),
        in_specs=[pl.BlockSpec(memory_space=pltpu.HBM)] * 2,
        out_specs=(vmem,) * 3,
        scratch_shapes=[
            pltpu.VMEM((2, ny, nz), f32),
            pltpu.VMEM((2, ny, nz), f32),
            pltpu.SemaphoreType.DMA((3,)),
        ],
        compiler_params=grant(4),
        name="pack",
    )(pltpu.with_memory_space_constraint(theta, pltpu.HBM), pltpu.with_memory_space_constraint(velocity, pltpu.HBM))

    def gathered(x):
        turns = [[((i + t) % ngrp, i) for i in range(ngrp)] for t in range(1, ngrp)]
        return [x] + [lax.ppermute(x, "grp", turn) for turn in turns]

    kappa = jnp.broadcast_to(diffusivity[:, None], (8, 128))
    part = lax.axis_index("grp").astype(jnp.int32)[None]
    left = lax.ppermute(tail, "slab", up)
    right = lax.ppermute(head, "slab", down)
    vel = gathered(own)
    gx, halo, tail, head = pl.pallas_call(
        first_kernel,
        out_shape=(full, jax.ShapeDtypeStruct((2, 4 * rows, nz), bf16), edge, edge),
        in_specs=[vmem] * 4,
        out_specs=(vmem,) * 4,
        scratch_shapes=[pltpu.VMEM((planes, ny, nz), f32)],
        compiler_params=grant(8),
        name="first",
    )(kappa, field, left, right)
    grad_l = lax.ppermute(tail, "slab", up)
    grad_r = lax.ppermute(head, "slab", down)
    halo = gathered(halo)
    acc, inner = pl.pallas_call(
        functools.partial(inner_kernel, ngrp),
        out_shape=(full, full),
        in_specs=[smem] + [vmem] * (9 + ngrp),
        out_specs=(vmem,) * 2,
        compiler_params=grant(14),
        name="inner",
    )(part, kappa, field, gx, *vel, ky, kz, ky2, kz2, ry, rz)
    new, kept = pl.pallas_call(
        functools.partial(final_kernel, ngrp),
        out_shape=(full, full),
        in_specs=[smem] + [vmem] * (13 + 2 * ngrp),
        out_specs=(pl.BlockSpec(memory_space=pltpu.HBM),) * 2,
        scratch_shapes=[
            pltpu.VMEM((planes, ny, nz), f32),
            pltpu.VMEM((planes, ny, nz), f32),
            pltpu.VMEM((planes + 4, ny, nz), f32),
            pltpu.VMEM((planes, ny, nz), f32),
            pltpu.SemaphoreType.DMA((2 * planes,)),
        ],
        compiler_params=grant(14),
        name="final",
    )(part, field, saved, acc, inner, gx, left, right, grad_l, grad_r, *vel, *halo, ky, kz, ry, rz)
    return (new[None], kept[None])


def solution(mesh):
    in_specs = (
        P("grp", "slab", None, None),
        P("grp", "slab", None, None),
        P(None, "slab", "grp", None),
        P("grp"),
    )
    out_specs = (P("grp", "slab", None, None), P("grp", "slab", None, None))
    return jax.shard_map(shards, mesh=mesh, in_specs=in_specs, out_specs=out_specs, check_vma=False)
```

```python
import functools

import jax
import jax.numpy as jnp
import numpy as np
from jax import lax
from jax.experimental import pallas as pl
from jax.experimental.pallas import tpu as pltpu
from jax.sharding import PartitionSpec as P

BLK = 32
ALPHA = 4.0 / 9.0
BETA = 1.0 / 36.0
COEF_A = 40.0 / 27.0
COEF_B = 25.0 / 54.0
RK_A = -5.0 / 9.0
RK_B = 15.0 / 16.0
STEP = 0.2
EVEN = (-0.0390625, 0.2734375, 0.8203125, -0.0546875)
ODD = (-0.0546875, 0.8203125, 0.2734375, -0.0390625)
MXU = 256


def band(count):
    eye = lambda k: np.eye(count, k=k)
    return eye(0) + ALPHA * (eye(1) + eye(-1)) + BETA * (eye(2) + eye(-2))


def blocked_operator(count, block):
    rhs = np.zeros((count, count))
    for i in range(count):
        for shift, coef in ((1, COEF_A / 2), (-1, -COEF_A / 2), (2, COEF_B / 4), (-2, -COEF_B / 4)):
            rhs[i, (i + shift) % count] += coef
    return np.kron(np.eye(count // block), np.linalg.inv(band(block))) @ rhs


def refine_operator(count):
    out = np.zeros((2 * count, count))
    for k in range(count):
        for t in range(4):
            out[2 * k, (k - 2 + t) % count] += EVEN[t]
            out[2 * k + 1, (k - 1 + t) % count] += ODD[t]
    return out


def split(x):
    hi = x.astype(jnp.bfloat16)
    return hi, (x - hi.astype(jnp.float32)).astype(jnp.bfloat16)


def host_split(x):
    x = jnp.asarray(np.asarray(x, np.float32))
    return jnp.stack(split(x))


def host_stack(x):
    hi, lo = host_split(x)
    return jnp.concatenate([hi, lo, hi], axis=1)


def dot(a, b):
    return jnp.dot(a, b, preferred_element_type=jnp.float32)


def dot3(a, b):
    return dot(a[0], b[0]) + (dot(a[0], b[1]) + dot(a[1], b[0]))


def widen(half):
    mid = half.shape[1] // 2
    return [jnp.concatenate([k, jnp.concatenate([k[mid:], k[:mid]], axis=0)], axis=1) for k in (half[0], half[1])]


def along_y(op, x, ny):
    out = []
    for top in range(0, x[0].shape[0], ny):
        hi, lo = x[0][top : top + ny], x[1][top : top + ny]
        out.append(dot(op[...], jnp.concatenate([hi, hi, lo], axis=0)))
    return jnp.concatenate(out, axis=0)


def banded_lu(count):
    m = band(count)
    for k in range(count):
        for i in range(k + 1, min(k + 3, count)):
            m[i, k] /= m[k, k]
            m[i, k + 1 : min(k + 3, count)] -= m[i, k] * m[k, k + 1 : min(k + 3, count)]
    return m


def x_derivative(get, put, work, planes):
    m = banded_lu(planes)
    ratio = (COEF_B / 4) / (COEF_A / 2)
    y1 = y2 = None
    for i in range(planes):
        y = (get(i + 1) - get(i - 1)) + ratio * (get(i + 2) - get(i - 2))
        if i >= 1:
            y = y - float(m[i, i - 1]) * y1
        if i >= 2:
            y = y - float(m[i, i - 2]) * y2
        work[i] = y
        y1, y2 = y, y1
    x1 = x2 = None
    for i in reversed(range(planes)):
        inv = 1.0 / m[i, i]
        x = work[i] * float(inv * COEF_A / 2)
        if i + 1 < planes:
            x = x - float(m[i, i + 1] * inv) * x1
        if i + 2 < planes:
            x = x - float(m[i, i + 2] * inv) * x2
        put(i, x)
        x1, x2 = x, x1


SLOTS = ((0, 0), (0, 1), (0, 2), (1, 0), (1, 1), (2, 0), (2, 1))
FIRST, COUNT = (0, 3, 5), (3, 2, 2)


def pack_kernel(code, theta, velocity, out_a, out_b, vel, low, high, sems):
    planes, ny, nz = theta.shape[1:]
    coarse, rows, nzc = velocity.shape[1:]
    copies = (
        pltpu.make_async_copy(theta.at[0, pl.ds(0, 2)], low, sems.at[0]),
        pltpu.make_async_copy(theta.at[0, pl.ds(planes - 2, 2)], high, sems.at[1]),
        pltpu.make_async_copy(velocity, vel, sems.at[2]),
    )
    for copy in copies:
        copy.start()
    for copy in copies:
        copy.wait()

    def fill(out, edge, upper):
        out[: 2 * ny] = edge[...].reshape(2 * ny, nz).astype(jnp.bfloat16)
        for q in range(8):
            c, k = SLOTS[min(q, 6)]
            k = coarse - COUNT[c] + k if upper else k
            top = 2 * ny + rows * (q // 2)
            out[top : top + rows, nzc * (q % 2) : nzc * (q % 2 + 1)] = vel[c, k]

    @pl.when(code[1] == 0)
    def _():
        fill(out_a, high, True)
        fill(out_b, low, False)

    @pl.when(code[1] != 0)
    def _():
        fill(out_a, low, False)
        fill(out_b, high, True)


def sides(code, got_a, got_b, edges, halo=None):
    ny, nz = edges.shape[1:]

    def fill(left, right):
        for k, got in enumerate((left, right)):
            edges[2 * k : 2 * k + 2] = got[: 2 * ny].reshape(2, ny, nz).astype(jnp.float32)
            if halo is not None:
                halo[k] = got[2 * ny :]

    @pl.when(code[1] == 0)
    def _():
        fill(got_b, got_a)

    @pl.when(code[1] != 0)
    def _():
        fill(got_a, got_b)


def padded(th, edges):
    planes = th.shape[0]

    def get(p):
        if p < 0:
            return edges[p + 2]
        if p >= planes:
            return edges[p - planes + 2]
        return th[p]

    return get


def first_kernel(code, kap, th, got_a, got_b, gx, halo, out_a, out_b, work, edges):
    planes, ny, nz = th.shape
    kappa = kap[0:1, 0:1]
    sides(code, got_a, got_b, edges, halo)

    def put(i, value):
        gx[i] = kappa * value

    x_derivative(padded(th, edges), put, work, planes)

    def fill(out, start):
        out[...] = gx[start : start + 2].reshape(2 * ny, nz).astype(jnp.bfloat16)

    @pl.when(code[1] == 0)
    def _():
        fill(out_a, planes - 2)
        fill(out_b, 0)

    @pl.when(code[1] != 0)
    def _():
        fill(out_a, 0)
        fill(out_b, planes - 2)


def flow_of(part, vel, halo, ry, rz):
    ngrp = len(vel)
    coarse, rows, nzc = vel[0].shape[1:]

    wide = ry[part[0]]
    deep = jnp.concatenate([rz[...], rz[...]], axis=0)
    nyc = rows * ngrp

    def plane(c, k):
        if 0 <= k < coarse:
            got = [vel[g][c, k] for g in range(ngrp)]
        else:
            q = FIRST[c] + (COUNT[c] + k if k < 0 else k - coarse)
            top = rows * (q // 2)
            side = 0 if k < 0 else 1
            got = [halo[g][side, top : top + rows, nzc * (q % 2) : nzc * (q % 2 + 1)] for g in range(ngrp)]
        return jnp.concatenate([v.astype(jnp.float32) for v in got], axis=0)

    def fine(c, p):
        k = p // 2
        coefs, start = (EVEN, k - 2) if p % 2 == 0 else (ODD, k - 1)
        total = coefs[0] * plane(c, start)
        for t in range(1, 4):
            total = total + coefs[t] * plane(c, start + t)
        return total

    def flow(c, which):
        x = split(jnp.concatenate([fine(c, p) for p in which], axis=0))
        z = split(dot(jnp.concatenate(x, axis=1), deep))
        tops = range(0, z[0].shape[0], nyc)
        pairs = [jnp.concatenate([h[t : t + nyc] for h in z], axis=0) for t in tops]
        return jnp.concatenate([dot(wide, pair) for pair in pairs], axis=0)

    return flow


def is_inner(g, per, planes):
    return g * per >= 4 and (g + 1) * per <= planes - 4


def cross(flow, th, ky, kz, g, per):
    ny, nz = th.shape[1:]
    which = range(g * per, (g + 1) * per)
    x = th[g * per : (g + 1) * per].reshape(per * ny, nz)
    fy = split(flow(1, which) * x)
    fz = split(flow(2, which) * x)
    return (along_y(ky, fy, ny) + dot3(fz, kz)).reshape(per, ny, nz)


def inner_kernel(ngrp, part, kap, th, gx, *refs):
    vel, (ky, kz, ky2, kz2, ry, rz, acc, flux) = refs[:ngrp], refs[ngrp:]
    planes, ny, nz = th.shape
    per = max(1, MXU // ny)
    kappa = kap[0:1, 0:1]
    kz, kz2 = widen(kz), widen(kz2)
    flow = flow_of(part, vel, None, ry, rz)
    for g in range(planes // per):
        at = slice(g * per, (g + 1) * per)
        x = split(th[at].reshape(per * ny, nz))
        value = (-kappa * (along_y(ky2, x, ny) + dot3(x, kz2))).reshape(per, ny, nz)
        if is_inner(g, per, planes):
            value = value + cross(flow, th, ky, kz, g, per)
            flux[at] = flow(0, range(g * per, (g + 1) * per)).reshape(per, ny, nz) * th[at] - gx[at]
        acc[at] = value


def final_kernel(ngrp, index, th, reg, part, inner, gx, ta, tb, ga, gb, *refs):
    vel, halo, (ky, kz, ry, rz, new_hbm, saved_hbm, new, saved, flux, acc, edges, grads, sems) = refs[:ngrp], refs[ngrp : 2 * ngrp], refs[2 * ngrp :]
    planes, ny, nz = th.shape
    per = max(1, MXU // ny)
    kz = widen(kz)
    flow = flow_of(index, vel, halo, ry, rz)
    sides(index, ta, tb, edges)
    sides(index, ga, gb, grads)
    get = padded(th, edges)
    outer = [g for g in range(planes // per) if not is_inner(g, per, planes)]
    for g in outer:
        acc[g * per : (g + 1) * per] = cross(flow, th, ky, kz, g, per) + part[g * per : (g + 1) * per]
    todo = [p for p in range(-2, planes + 2) if not is_inner(p // per, per, planes)]
    for start in range(0, len(todo), per):
        which = todo[start : start + per]
        f = flow(0, which + which[:1] * (per - len(which))).reshape(per, ny, nz)
        for i, p in enumerate(which):
            if p < 0:
                d = grads[p + 2]
            elif p >= planes:
                d = grads[p - planes + 2]
            else:
                d = gx[p]
            flux[p + 2] = f[i] * get(p) - d

    def flux_at(p):
        return inner[p] if is_inner(p // per, per, planes) else flux[p + 2]

    def put(i, value):
        rest = part[i] if is_inner(i // per, per, planes) else acc[i]
        kept = RK_A * reg[i] - STEP * (value + rest)
        saved[i] = kept
        new[i] = th[i] + RK_B * kept
        if i % per == 0:
            at = pl.ds(i, per)
            for k, (src, dst) in enumerate(((saved, saved_hbm), (new, new_hbm))):
                copies.append(pltpu.make_async_copy(src.at[at], dst.at[at], sems.at[2 * (i // per) + k]))
                copies[-1].start()

    copies = []
    x_derivative(flux_at, put, saved, planes)
    for copy in copies:
        copy.wait()


def shards(theta, register, velocity, diffusivity):
    planes, ny, nz = theta.shape[1:]
    nslab, ngrp = lax.axis_size("slab"), lax.axis_size("grp")
    nyc, nzc = ny // 2, nz // 2
    f32, bf16 = jnp.float32, jnp.bfloat16
    swap_a = [(i, i + 1 - 2 * (i % 2)) for i in range(nslab)]
    swap_b = [(i, (i - 1 + 2 * (i % 2)) % nslab) for i in range(nslab)]
    op_y, op_z = blocked_operator(ny, BLK), blocked_operator(nz, BLK)
    ky2, kz2 = host_stack(op_y @ op_y), host_split((op_z @ op_z).T[:, : nz // 2])
    ky, kz = host_stack(op_y), host_split(op_z.T[:, : nz // 2])
    turned = [np.roll(refine_operator(nyc), -g * (nyc // ngrp), axis=1) for g in range(ngrp)]
    ry = jnp.asarray(np.stack([np.tile(m, (1, 2)) for m in turned]), bf16)
    rz = jnp.asarray(refine_operator(nzc).T, bf16)

    field, saved = theta[0], register[0]
    rows, coarse = velocity.shape[2], planes // 2
    full = jax.ShapeDtypeStruct((planes, ny, nz), f32)
    edge = jax.ShapeDtypeStruct((2 * ny, nz), bf16)
    packed = jax.ShapeDtypeStruct((2 * ny + 4 * rows, nz), bf16)
    vmem = pl.BlockSpec(memory_space=pltpu.VMEM)
    smem = pl.BlockSpec(memory_space=pltpu.SMEM)
    grant = lambda mib: pltpu.CompilerParams(vmem_limit_bytes=mib * 1024 * 1024)

    part = jnp.stack([lax.axis_index("grp"), lax.axis_index("slab") % 2]).astype(jnp.int32)
    out_a, out_b, own = pl.pallas_call(
        pack_kernel,
        out_shape=(packed, packed, jax.ShapeDtypeStruct(velocity.shape, bf16)),
        in_specs=[smem] + [pl.BlockSpec(memory_space=pltpu.HBM)] * 2,
        out_specs=(vmem,) * 3,
        scratch_shapes=[
            pltpu.VMEM((2, ny, nz), f32),
            pltpu.VMEM((2, ny, nz), f32),
            pltpu.SemaphoreType.DMA((3,)),
        ],
        compiler_params=grant(4),
        name="pack",
    )(part, pltpu.with_memory_space_constraint(theta, pltpu.HBM), pltpu.with_memory_space_constraint(velocity, pltpu.HBM))

    def gathered(x):
        turns = [[((i + t) % ngrp, i) for i in range(ngrp)] for t in range(1, ngrp)]
        return [x] + [lax.ppermute(x, "grp", turn) for turn in turns]

    kappa = jnp.broadcast_to(diffusivity[:, None], (8, 128))
    got_a = lax.ppermute(out_a, "slab", swap_a)
    got_b = lax.ppermute(out_b, "slab", swap_b)
    vel = gathered(own)
    gx, halo, out_a, out_b = pl.pallas_call(
        first_kernel,
        out_shape=(full, jax.ShapeDtypeStruct((2, 4 * rows, nz), bf16), edge, edge),
        in_specs=[smem] + [vmem] * 4,
        out_specs=(vmem,) * 4,
        scratch_shapes=[pltpu.VMEM((planes, ny, nz), f32), pltpu.VMEM((4, ny, nz), f32)],
        compiler_params=grant(8),
        name="first",
    )(part, kappa, field, got_a, got_b)
    grad_a = lax.ppermute(out_a, "slab", swap_a)
    grad_b = lax.ppermute(out_b, "slab", swap_b)
    halo = gathered(halo)
    acc, inner = pl.pallas_call(
        functools.partial(inner_kernel, ngrp),
        out_shape=(full, full),
        in_specs=[smem] + [vmem] * (9 + ngrp),
        out_specs=(vmem,) * 2,
        compiler_params=grant(14),
        name="inner",
    )(part, kappa, field, gx, *vel, ky, kz, ky2, kz2, ry, rz)
    new, kept = pl.pallas_call(
        functools.partial(final_kernel, ngrp),
        out_shape=(full, full),
        in_specs=[smem] + [vmem] * (13 + 2 * ngrp),
        out_specs=(pl.BlockSpec(memory_space=pltpu.HBM),) * 2,
        scratch_shapes=[
            pltpu.VMEM((planes, ny, nz), f32),
            pltpu.VMEM((planes, ny, nz), f32),
            pltpu.VMEM((planes + 4, ny, nz), f32),
            pltpu.VMEM((planes, ny, nz), f32),
            pltpu.VMEM((4, ny, nz), f32),
            pltpu.VMEM((4, ny, nz), f32),
            pltpu.SemaphoreType.DMA((2 * planes,)),
        ],
        compiler_params=grant(14),
        name="final",
    )(part, field, saved, acc, inner, gx, got_a, got_b, grad_a, grad_b, *vel, *halo, ky, kz, ry, rz)
    return (new[None], kept[None])


def solution(mesh):
    in_specs = (
        P("grp", "slab", None, None),
        P("grp", "slab", None, None),
        P(None, "slab", "grp", None),
        P("grp"),
    )
    out_specs = (P("grp", "slab", None, None), P("grp", "slab", None, None))
    return jax.shard_map(shards, mesh=mesh, in_specs=in_specs, out_specs=out_specs, check_vma=False)
```

```python
import functools

import jax
import jax.numpy as jnp
import numpy as np
from jax import lax
from jax.experimental import pallas as pl
from jax.experimental.pallas import tpu as pltpu
from jax.sharding import PartitionSpec as P

BLK = 32
ALPHA = 4.0 / 9.0
BETA = 1.0 / 36.0
COEF_A = 40.0 / 27.0
COEF_B = 25.0 / 54.0
RK_A = -5.0 / 9.0
RK_B = 15.0 / 16.0
STEP = 0.2
EVEN = (-0.0390625, 0.2734375, 0.8203125, -0.0546875)
ODD = (-0.0546875, 0.8203125, 0.2734375, -0.0390625)
MXU = 256


def band(count):
    eye = lambda k: np.eye(count, k=k)
    return eye(0) + ALPHA * (eye(1) + eye(-1)) + BETA * (eye(2) + eye(-2))


def blocked_operator(count, block):
    rhs = np.zeros((count, count))
    for i in range(count):
        for shift, coef in ((1, COEF_A / 2), (-1, -COEF_A / 2), (2, COEF_B / 4), (-2, -COEF_B / 4)):
            rhs[i, (i + shift) % count] += coef
    return np.kron(np.eye(count // block), np.linalg.inv(band(block))) @ rhs


def refine_operator(count):
    out = np.zeros((2 * count, count))
    for k in range(count):
        for t in range(4):
            out[2 * k, (k - 2 + t) % count] += EVEN[t]
            out[2 * k + 1, (k - 1 + t) % count] += ODD[t]
    return out


def split(x):
    hi = x.astype(jnp.bfloat16)
    return hi, (x - hi.astype(jnp.float32)).astype(jnp.bfloat16)


def host_split(x):
    x = jnp.asarray(np.asarray(x, np.float32))
    return jnp.stack(split(x))


def host_stack(x):
    hi, lo = host_split(x)
    return jnp.concatenate([hi, lo, hi], axis=1)


def dot(a, b):
    return jnp.dot(a, b, preferred_element_type=jnp.float32)


def dot3(a, b):
    return dot(a[0], b[0]) + (dot(a[0], b[1]) + dot(a[1], b[0]))


def widen(half):
    mid = half.shape[1] // 2
    return [jnp.concatenate([k, jnp.concatenate([k[mid:], k[:mid]], axis=0)], axis=1) for k in (half[0], half[1])]


def along_y(op, x, ny):
    out = []
    for top in range(0, x[0].shape[0], ny):
        hi, lo = x[0][top : top + ny], x[1][top : top + ny]
        out.append(dot(op[...], jnp.concatenate([hi, hi, lo], axis=0)))
    return jnp.concatenate(out, axis=0)


def banded_lu(count):
    m = band(count)
    for k in range(count):
        for i in range(k + 1, min(k + 3, count)):
            m[i, k] /= m[k, k]
            m[i, k + 1 : min(k + 3, count)] -= m[i, k] * m[k, k + 1 : min(k + 3, count)]
    return m


def x_derivative(get, put, work, planes):
    m = banded_lu(planes)
    ratio = (COEF_B / 4) / (COEF_A / 2)
    y1 = y2 = None
    for i in range(planes):
        y = (get(i + 1) - get(i - 1)) + ratio * (get(i + 2) - get(i - 2))
        if i >= 1:
            y = y - float(m[i, i - 1]) * y1
        if i >= 2:
            y = y - float(m[i, i - 2]) * y2
        work[i] = y
        y1, y2 = y, y1
    x1 = x2 = None
    for i in reversed(range(planes)):
        inv = 1.0 / m[i, i]
        x = work[i] * float(inv * COEF_A / 2)
        if i + 1 < planes:
            x = x - float(m[i, i + 1] * inv) * x1
        if i + 2 < planes:
            x = x - float(m[i, i + 2] * inv) * x2
        put(i, x)
        x1, x2 = x, x1


SLOTS = ((0, 0), (0, 1), (0, 2), (1, 0), (1, 1), (2, 0), (2, 1))
FIRST, COUNT = (0, 3, 5), (3, 2, 2)


def pack_kernel(code, theta, velocity, out_a, out_b, vel, low, high, sems):
    planes, ny, nz = theta.shape[1:]
    coarse, rows, nzc = velocity.shape[1:]
    copies = (
        pltpu.make_async_copy(theta.at[0, pl.ds(0, 2)], low, sems.at[0]),
        pltpu.make_async_copy(theta.at[0, pl.ds(planes - 2, 2)], high, sems.at[1]),
        pltpu.make_async_copy(velocity, vel, sems.at[2]),
    )
    for copy in copies:
        copy.start()
    for copy in copies:
        copy.wait()

    def fill(out, edge, upper):
        out[: 2 * ny] = edge[...].reshape(2 * ny, nz).astype(jnp.bfloat16)
        for q in range(8):
            c, k = SLOTS[min(q, 6)]
            k = coarse - COUNT[c] + k if upper else k
            top = 2 * ny + rows * (q // 2)
            out[top : top + rows, nzc * (q % 2) : nzc * (q % 2 + 1)] = vel[c, k]

    @pl.when((code[0] & 1) == 0)
    def _():
        fill(out_a, high, True)
        fill(out_b, low, False)

    @pl.when((code[0] & 1) != 0)
    def _():
        fill(out_a, low, False)
        fill(out_b, high, True)


def sides(code, got_a, got_b, edges, halo=None):
    ny, nz = edges.shape[1:]

    def fill(left, right):
        for k, got in enumerate((left, right)):
            edges[2 * k : 2 * k + 2] = got[: 2 * ny].reshape(2, ny, nz).astype(jnp.float32)
            if halo is not None:
                halo[k] = got[2 * ny :]

    @pl.when((code[0] & 1) == 0)
    def _():
        fill(got_b, got_a)

    @pl.when((code[0] & 1) != 0)
    def _():
        fill(got_a, got_b)


def padded(th, edges):
    planes = th.shape[0]

    def get(p):
        if p < 0:
            return edges[p + 2]
        if p >= planes:
            return edges[p - planes + 2]
        return th[p]

    return get


def first_kernel(code, kap, th, got_a, got_b, gx, halo, out_a, out_b, work, edges):
    planes, ny, nz = th.shape
    kappa = kap[0:1, 0:1]
    sides(code, got_a, got_b, edges, halo)

    def put(i, value):
        gx[i] = kappa * value

    x_derivative(padded(th, edges), put, work, planes)

    def fill(out, start):
        out[...] = gx[start : start + 2].reshape(2 * ny, nz).astype(jnp.bfloat16)

    @pl.when((code[0] & 1) == 0)
    def _():
        fill(out_a, planes - 2)
        fill(out_b, 0)

    @pl.when((code[0] & 1) != 0)
    def _():
        fill(out_a, 0)
        fill(out_b, planes - 2)


def flow_of(part, vel, halo, ry, rz):
    ngrp = len(vel)
    coarse, rows, nzc = vel[0].shape[1:]

    wide = ry[part[0] >> 1]
    deep = jnp.concatenate([rz[...], rz[...]], axis=0)
    nyc = rows * ngrp

    def plane(c, k):
        if 0 <= k < coarse:
            got = [vel[g][c, k] for g in range(ngrp)]
        else:
            q = FIRST[c] + (COUNT[c] + k if k < 0 else k - coarse)
            top = rows * (q // 2)
            side = 0 if k < 0 else 1
            got = [halo[g][side, top : top + rows, nzc * (q % 2) : nzc * (q % 2 + 1)] for g in range(ngrp)]
        return jnp.concatenate([v.astype(jnp.float32) for v in got], axis=0)

    def fine(c, p):
        k = p // 2
        coefs, start = (EVEN, k - 2) if p % 2 == 0 else (ODD, k - 1)
        total = coefs[0] * plane(c, start)
        for t in range(1, 4):
            total = total + coefs[t] * plane(c, start + t)
        return total

    def flow(c, which):
        x = split(jnp.concatenate([fine(c, p) for p in which], axis=0))
        z = split(dot(jnp.concatenate(x, axis=1), deep))
        tops = range(0, z[0].shape[0], nyc)
        pairs = [jnp.concatenate([h[t : t + nyc] for h in z], axis=0) for t in tops]
        return jnp.concatenate([dot(wide, pair) for pair in pairs], axis=0)

    return flow


def is_inner(g, per, planes):
    return g * per >= 4 and (g + 1) * per <= planes - 4


def cross(flow, th, ky, kz, g, per):
    ny, nz = th.shape[1:]
    which = range(g * per, (g + 1) * per)
    x = th[g * per : (g + 1) * per].reshape(per * ny, nz)
    fy = split(flow(1, which) * x)
    fz = split(flow(2, which) * x)
    return (along_y(ky, fy, ny) + dot3(fz, kz)).reshape(per, ny, nz)


def inner_kernel(ngrp, part, kap, th, gx, *refs):
    vel, (ky, kz, ky2, kz2, ry, rz, acc, flux) = refs[:ngrp], refs[ngrp:]
    planes, ny, nz = th.shape
    per = max(1, MXU // ny)
    kappa = kap[0:1, 0:1]
    kz, kz2 = widen(kz), widen(kz2)
    flow = flow_of(part, vel, None, ry, rz)
    for g in range(planes // per):
        at = slice(g * per, (g + 1) * per)
        x = split(th[at].reshape(per * ny, nz))
        value = (-kappa * (along_y(ky2, x, ny) + dot3(x, kz2))).reshape(per, ny, nz)
        if is_inner(g, per, planes):
            value = value + cross(flow, th, ky, kz, g, per)
            flux[at] = flow(0, range(g * per, (g + 1) * per)).reshape(per, ny, nz) * th[at] - gx[at]
        acc[at] = value


def final_kernel(ngrp, index, th, reg, part, inner, gx, ta, tb, ga, gb, *refs):
    vel, halo, (ky, kz, ry, rz, new_hbm, saved_hbm, new, saved, flux, acc, edges, grads, sems) = refs[:ngrp], refs[ngrp : 2 * ngrp], refs[2 * ngrp :]
    planes, ny, nz = th.shape
    per = max(1, MXU // ny)
    kz = widen(kz)
    flow = flow_of(index, vel, halo, ry, rz)
    sides(index, ta, tb, edges)
    sides(index, ga, gb, grads)
    get = padded(th, edges)
    outer = [g for g in range(planes // per) if not is_inner(g, per, planes)]
    for g in outer:
        acc[g * per : (g + 1) * per] = cross(flow, th, ky, kz, g, per) + part[g * per : (g + 1) * per]
    todo = [p for p in range(-2, planes + 2) if not is_inner(p // per, per, planes)]
    for start in range(0, len(todo), per):
        which = todo[start : start + per]
        f = flow(0, which + which[:1] * (per - len(which))).reshape(per, ny, nz)
        for i, p in enumerate(which):
            if p < 0:
                d = grads[p + 2]
            elif p >= planes:
                d = grads[p - planes + 2]
            else:
                d = gx[p]
            flux[p + 2] = f[i] * get(p) - d

    def flux_at(p):
        return inner[p] if is_inner(p // per, per, planes) else flux[p + 2]

    def put(i, value):
        rest = part[i] if is_inner(i // per, per, planes) else acc[i]
        kept = RK_A * reg[i] - STEP * (value + rest)
        saved[i] = kept
        new[i] = th[i] + RK_B * kept
        if i % per == 0:
            at = pl.ds(i, per)
            for k, (src, dst) in enumerate(((saved, saved_hbm), (new, new_hbm))):
                copies.append(pltpu.make_async_copy(src.at[at], dst.at[at], sems.at[2 * (i // per) + k]))
                copies[-1].start()

    copies = []
    x_derivative(flux_at, put, saved, planes)
    for copy in copies:
        copy.wait()


def shards(theta, register, velocity, diffusivity):
    planes, ny, nz = theta.shape[1:]
    nslab, ngrp = lax.axis_size("slab"), lax.axis_size("grp")
    nyc, nzc = ny // 2, nz // 2
    f32, bf16 = jnp.float32, jnp.bfloat16
    swap_a = [(i, i + 1 - 2 * (i % 2)) for i in range(nslab)]
    swap_b = [(i, (i - 1 + 2 * (i % 2)) % nslab) for i in range(nslab)]
    op_y, op_z = blocked_operator(ny, BLK), blocked_operator(nz, BLK)
    ky2, kz2 = host_stack(op_y @ op_y), host_split((op_z @ op_z).T[:, : nz // 2])
    ky, kz = host_stack(op_y), host_split(op_z.T[:, : nz // 2])
    turned = [np.roll(refine_operator(nyc), -g * (nyc // ngrp), axis=1) for g in range(ngrp)]
    ry = jnp.asarray(np.stack([np.tile(m, (1, 2)) for m in turned]), bf16)
    rz = jnp.asarray(refine_operator(nzc).T, bf16)

    field, saved = theta[0], register[0]
    rows, coarse = velocity.shape[2], planes // 2
    full = jax.ShapeDtypeStruct((planes, ny, nz), f32)
    edge = jax.ShapeDtypeStruct((2 * ny, nz), bf16)
    packed = jax.ShapeDtypeStruct((2 * ny + 4 * rows, nz), bf16)
    vmem = pl.BlockSpec(memory_space=pltpu.VMEM)
    smem = pl.BlockSpec(memory_space=pltpu.SMEM)
    grant = lambda mib: pltpu.CompilerParams(vmem_limit_bytes=mib * 1024 * 1024)

    part = (lax.axis_index("grp") * 2 + lax.axis_index("slab") % 2).astype(jnp.int32)[None]
    out_a, out_b, own = pl.pallas_call(
        pack_kernel,
        out_shape=(packed, packed, jax.ShapeDtypeStruct(velocity.shape, bf16)),
        in_specs=[smem] + [pl.BlockSpec(memory_space=pltpu.HBM)] * 2,
        out_specs=(vmem,) * 3,
        scratch_shapes=[
            pltpu.VMEM((2, ny, nz), f32),
            pltpu.VMEM((2, ny, nz), f32),
            pltpu.SemaphoreType.DMA((3,)),
        ],
        compiler_params=grant(4),
        name="pack",
    )(part, pltpu.with_memory_space_constraint(theta, pltpu.HBM), pltpu.with_memory_space_constraint(velocity, pltpu.HBM))

    def gathered(x):
        turns = [[((i + t) % ngrp, i) for i in range(ngrp)] for t in range(1, ngrp)]
        return [x] + [lax.ppermute(x, "grp", turn) for turn in turns]

    kappa = jnp.broadcast_to(diffusivity[:, None], (8, 128))
    got_a = lax.ppermute(out_a, "slab", swap_a)
    got_b = lax.ppermute(out_b, "slab", swap_b)
    vel = gathered(own)
    gx, halo, out_a, out_b = pl.pallas_call(
        first_kernel,
        out_shape=(full, jax.ShapeDtypeStruct((2, 4 * rows, nz), bf16), edge, edge),
        in_specs=[smem] + [vmem] * 4,
        out_specs=(vmem,) * 4,
        scratch_shapes=[pltpu.VMEM((planes, ny, nz), f32), pltpu.VMEM((4, ny, nz), f32)],
        compiler_params=grant(8),
        name="first",
    )(part, kappa, field, got_a, got_b)
    grad_a = lax.ppermute(out_a, "slab", swap_a)
    grad_b = lax.ppermute(out_b, "slab", swap_b)
    halo = gathered(halo)
    acc, inner = pl.pallas_call(
        functools.partial(inner_kernel, ngrp),
        out_shape=(full, full),
        in_specs=[smem] + [vmem] * (9 + ngrp),
        out_specs=(vmem,) * 2,
        compiler_params=grant(14),
        name="inner",
    )(part, kappa, field, gx, *vel, ky, kz, ky2, kz2, ry, rz)
    new, kept = pl.pallas_call(
        functools.partial(final_kernel, ngrp),
        out_shape=(full, full),
        in_specs=[smem] + [vmem] * (13 + 2 * ngrp),
        out_specs=(pl.BlockSpec(memory_space=pltpu.HBM),) * 2,
        scratch_shapes=[
            pltpu.VMEM((planes, ny, nz), f32),
            pltpu.VMEM((planes, ny, nz), f32),
            pltpu.VMEM((planes + 4, ny, nz), f32),
            pltpu.VMEM((planes, ny, nz), f32),
            pltpu.VMEM((4, ny, nz), f32),
            pltpu.VMEM((4, ny, nz), f32),
            pltpu.SemaphoreType.DMA((2 * planes,)),
        ],
        compiler_params=grant(14),
        name="final",
    )(part, field, saved, acc, inner, gx, got_a, got_b, grad_a, grad_b, *vel, *halo, ky, kz, ry, rz)
    return (new[None], kept[None])


def solution(mesh):
    in_specs = (
        P("grp", "slab", None, None),
        P("grp", "slab", None, None),
        P(None, "slab", "grp", None),
        P("grp"),
    )
    out_specs = (P("grp", "slab", None, None), P("grp", "slab", None, None))
    return jax.shard_map(shards, mesh=mesh, in_specs=in_specs, out_specs=out_specs, check_vma=False)
```

```python
import functools

import jax
import jax.numpy as jnp
import numpy as np
from jax import lax
from jax.experimental import pallas as pl
from jax.experimental.pallas import tpu as pltpu
from jax.sharding import PartitionSpec as P

BLK = 32
ALPHA = 4.0 / 9.0
BETA = 1.0 / 36.0
COEF_A = 40.0 / 27.0
COEF_B = 25.0 / 54.0
RK_A = -5.0 / 9.0
RK_B = 15.0 / 16.0
STEP = 0.2
EVEN = (-0.0390625, 0.2734375, 0.8203125, -0.0546875)
ODD = (-0.0546875, 0.8203125, 0.2734375, -0.0390625)
MXU = 256


def band(count):
    eye = lambda k: np.eye(count, k=k)
    return eye(0) + ALPHA * (eye(1) + eye(-1)) + BETA * (eye(2) + eye(-2))


def blocked_operator(count, block):
    rhs = np.zeros((count, count))
    for i in range(count):
        for shift, coef in ((1, COEF_A / 2), (-1, -COEF_A / 2), (2, COEF_B / 4), (-2, -COEF_B / 4)):
            rhs[i, (i + shift) % count] += coef
    return np.kron(np.eye(count // block), np.linalg.inv(band(block))) @ rhs


def refine_operator(count):
    out = np.zeros((2 * count, count))
    for k in range(count):
        for t in range(4):
            out[2 * k, (k - 2 + t) % count] += EVEN[t]
            out[2 * k + 1, (k - 1 + t) % count] += ODD[t]
    return out


def split(x):
    hi = x.astype(jnp.bfloat16)
    return hi, (x - hi.astype(jnp.float32)).astype(jnp.bfloat16)


def host_split(x):
    x = jnp.asarray(np.asarray(x, np.float32))
    return jnp.stack(split(x))


def host_stack(x):
    hi, lo = host_split(x)
    return jnp.concatenate([hi, lo, hi], axis=1)


def dot(a, b):
    return jnp.dot(a, b, preferred_element_type=jnp.float32)


def dot3(a, b):
    return dot(a[0], b[0]) + (dot(a[0], b[1]) + dot(a[1], b[0]))


def widen(half):
    mid = half.shape[1] // 2
    return [jnp.concatenate([k, jnp.concatenate([k[mid:], k[:mid]], axis=0)], axis=1) for k in (half[0], half[1])]


def along_y(op, x, ny):
    out = []
    for top in range(0, x[0].shape[0], ny):
        hi, lo = x[0][top : top + ny], x[1][top : top + ny]
        out.append(dot(op[...], jnp.concatenate([hi, hi, lo], axis=0)))
    return jnp.concatenate(out, axis=0)


def banded_lu(count):
    m = band(count)
    for k in range(count):
        for i in range(k + 1, min(k + 3, count)):
            m[i, k] /= m[k, k]
            m[i, k + 1 : min(k + 3, count)] -= m[i, k] * m[k, k + 1 : min(k + 3, count)]
    return m


def x_derivative(get_at, put_at, work, planes):
    ny = work.shape[1]
    for top in range(0, ny, BLK):
        rows = slice(top, top + BLK)
        x_rows(lambda p: get_at(p, rows), lambda i, v: put_at(i, v, rows), work.at[:, rows], planes)


def x_rows(get, put, work, planes):
    m = banded_lu(planes)
    ratio = (COEF_B / 4) / (COEF_A / 2)
    y1 = y2 = None
    for i in range(planes):
        y = (get(i + 1) - get(i - 1)) + ratio * (get(i + 2) - get(i - 2))
        if i >= 1:
            y = y - float(m[i, i - 1]) * y1
        if i >= 2:
            y = y - float(m[i, i - 2]) * y2
        work[i] = y
        y1, y2 = y, y1
    x1 = x2 = None
    for i in reversed(range(planes)):
        inv = 1.0 / m[i, i]
        x = work[i] * float(inv * COEF_A / 2)
        if i + 1 < planes:
            x = x - float(m[i, i + 1] * inv) * x1
        if i + 2 < planes:
            x = x - float(m[i, i + 2] * inv) * x2
        put(i, x)
        x1, x2 = x, x1


SLOTS = ((0, 0), (0, 1), (0, 2), (1, 0), (1, 1), (2, 0), (2, 1))
FIRST, COUNT = (0, 3, 5), (3, 2, 2)


def pack_kernel(code, theta, velocity, out_a, out_b, vel, low, high, sems):
    planes, ny, nz = theta.shape[1:]
    coarse, rows, nzc = velocity.shape[1:]
    copies = (
        pltpu.make_async_copy(theta.at[0, pl.ds(0, 2)], low, sems.at[0]),
        pltpu.make_async_copy(theta.at[0, pl.ds(planes - 2, 2)], high, sems.at[1]),
        pltpu.make_async_copy(velocity, vel, sems.at[2]),
    )
    for copy in copies:
        copy.start()
    for copy in copies:
        copy.wait()

    def fill(out, edge, upper):
        out[: 2 * ny] = edge[...].reshape(2 * ny, nz).astype(jnp.bfloat16)
        for q in range(8):
            c, k = SLOTS[min(q, 6)]
            k = coarse - COUNT[c] + k if upper else k
            top = 2 * ny + rows * (q // 2)
            out[top : top + rows, nzc * (q % 2) : nzc * (q % 2 + 1)] = vel[c, k]

    @pl.when((code[0] & 1) == 0)
    def _():
        fill(out_a, high, True)
        fill(out_b, low, False)

    @pl.when((code[0] & 1) != 0)
    def _():
        fill(out_a, low, False)
        fill(out_b, high, True)


def sides(code, got_a, got_b, edges, halo=None):
    ny, nz = edges.shape[1:]

    def fill(left, right):
        for k, got in enumerate((left, right)):
            edges[2 * k : 2 * k + 2] = got[: 2 * ny].reshape(2, ny, nz).astype(jnp.float32)
            if halo is not None:
                halo[k] = got[2 * ny :]

    @pl.when((code[0] & 1) == 0)
    def _():
        fill(got_b, got_a)

    @pl.when((code[0] & 1) != 0)
    def _():
        fill(got_a, got_b)


def padded(th, edges):
    planes = th.shape[0]

    def get(p, rows=slice(None)):
        if p < 0:
            return edges[p + 2, rows]
        if p >= planes:
            return edges[p - planes + 2, rows]
        return th[p, rows]

    return get


def first_kernel(code, kap, th, got_a, got_b, gx, halo, out_a, out_b, work, edges):
    planes, ny, nz = th.shape
    kappa = kap[0:1, 0:1]
    sides(code, got_a, got_b, edges, halo)

    def put(i, value, rows):
        gx[i, rows] = kappa * value

    x_derivative(padded(th, edges), put, work, planes)

    def fill(out, start):
        out[...] = gx[start : start + 2].reshape(2 * ny, nz).astype(jnp.bfloat16)

    @pl.when((code[0] & 1) == 0)
    def _():
        fill(out_a, planes - 2)
        fill(out_b, 0)

    @pl.when((code[0] & 1) != 0)
    def _():
        fill(out_a, 0)
        fill(out_b, planes - 2)


def flow_of(part, vel, halo, ry, rz):
    ngrp = len(vel)
    coarse, rows, nzc = vel[0].shape[1:]

    wide = ry[part[0] >> 1]
    deep = jnp.concatenate([rz[...], rz[...]], axis=0)
    nyc = rows * ngrp

    def plane(c, k):
        if 0 <= k < coarse:
            got = [vel[g][c, k] for g in range(ngrp)]
        else:
            q = FIRST[c] + (COUNT[c] + k if k < 0 else k - coarse)
            top = rows * (q // 2)
            side = 0 if k < 0 else 1
            got = [halo[g][side, top : top + rows, nzc * (q % 2) : nzc * (q % 2 + 1)] for g in range(ngrp)]
        return jnp.concatenate([v.astype(jnp.float32) for v in got], axis=0)

    def fine(c, p):
        k = p // 2
        coefs, start = (EVEN, k - 2) if p % 2 == 0 else (ODD, k - 1)
        total = coefs[0] * plane(c, start)
        for t in range(1, 4):
            total = total + coefs[t] * plane(c, start + t)
        return total

    def flow(c, which):
        x = split(jnp.concatenate([fine(c, p) for p in which], axis=0))
        z = split(dot(jnp.concatenate(x, axis=1), deep))
        tops = range(0, z[0].shape[0], nyc)
        pairs = [jnp.concatenate([h[t : t + nyc] for h in z], axis=0) for t in tops]
        return jnp.concatenate([dot(wide, pair) for pair in pairs], axis=0)

    return flow


def is_inner(g, per, planes):
    return g * per >= 4 and (g + 1) * per <= planes - 4


def cross(flow, th, ky, kz, g, per):
    ny, nz = th.shape[1:]
    which = range(g * per, (g + 1) * per)
    x = th[g * per : (g + 1) * per].reshape(per * ny, nz)
    fy = split(flow(1, which) * x)
    fz = split(flow(2, which) * x)
    return (along_y(ky, fy, ny) + dot3(fz, kz)).reshape(per, ny, nz)


def inner_kernel(ngrp, part, kap, th, gx, *refs):
    vel, (ky, kz, ky2, kz2, ry, rz, acc, flux) = refs[:ngrp], refs[ngrp:]
    planes, ny, nz = th.shape
    per = max(1, MXU // ny)
    kappa = kap[0:1, 0:1]
    kz, kz2 = widen(kz), widen(kz2)
    flow = flow_of(part, vel, None, ry, rz)
    for g in range(planes // per):
        at = slice(g * per, (g + 1) * per)
        x = split(th[at].reshape(per * ny, nz))
        value = (-kappa * (along_y(ky2, x, ny) + dot3(x, kz2))).reshape(per, ny, nz)
        if is_inner(g, per, planes):
            value = value + cross(flow, th, ky, kz, g, per)
            flux[at] = flow(0, range(g * per, (g + 1) * per)).reshape(per, ny, nz) * th[at] - gx[at]
        acc[at] = value


def final_kernel(ngrp, index, th, reg, part, inner, gx, ta, tb, ga, gb, *refs):
    vel, halo, (ky, kz, ry, rz, new_hbm, saved_hbm, new, saved, flux, acc, edges, grads, sems) = refs[:ngrp], refs[ngrp : 2 * ngrp], refs[2 * ngrp :]
    planes, ny, nz = th.shape
    per = max(1, MXU // ny)
    kz = widen(kz)
    flow = flow_of(index, vel, halo, ry, rz)
    sides(index, ta, tb, edges)
    sides(index, ga, gb, grads)
    get = padded(th, edges)
    outer = [g for g in range(planes // per) if not is_inner(g, per, planes)]
    for g in outer:
        acc[g * per : (g + 1) * per] = cross(flow, th, ky, kz, g, per) + part[g * per : (g + 1) * per]
    todo = [p for p in range(-2, planes + 2) if not is_inner(p // per, per, planes)]
    for start in range(0, len(todo), per):
        which = todo[start : start + per]
        f = flow(0, which + which[:1] * (per - len(which))).reshape(per, ny, nz)
        for i, p in enumerate(which):
            if p < 0:
                d = grads[p + 2]
            elif p >= planes:
                d = grads[p - planes + 2]
            else:
                d = gx[p]
            flux[p + 2] = f[i] * get(p) - d

    def flux_at(p, rows):
        return inner[p, rows] if is_inner(p // per, per, planes) else flux[p + 2, rows]

    def put(i, value, rows):
        rest = part[i, rows] if is_inner(i // per, per, planes) else acc[i, rows]
        kept = RK_A * reg[i, rows] - STEP * (value + rest)
        saved[i, rows] = kept
        new[i, rows] = th[i, rows] + RK_B * kept
        if i % per == 0:
            at = (pl.ds(i, per), pl.ds(rows.start, BLK))
            for src, dst in ((saved, saved_hbm), (new, new_hbm)):
                copies.append(pltpu.make_async_copy(src.at[at], dst.at[at], sems.at[len(copies)]))
                copies[-1].start()

    copies = []
    x_derivative(flux_at, put, saved, planes)
    for copy in copies:
        copy.wait()


def shards(theta, register, velocity, diffusivity):
    planes, ny, nz = theta.shape[1:]
    nslab, ngrp = lax.axis_size("slab"), lax.axis_size("grp")
    nyc, nzc = ny // 2, nz // 2
    f32, bf16 = jnp.float32, jnp.bfloat16
    swap_a = [(i, i + 1 - 2 * (i % 2)) for i in range(nslab)]
    swap_b = [(i, (i - 1 + 2 * (i % 2)) % nslab) for i in range(nslab)]
    op_y, op_z = blocked_operator(ny, BLK), blocked_operator(nz, BLK)
    ky2, kz2 = host_stack(op_y @ op_y), host_split((op_z @ op_z).T[:, : nz // 2])
    ky, kz = host_stack(op_y), host_split(op_z.T[:, : nz // 2])
    turned = [np.roll(refine_operator(nyc), -g * (nyc // ngrp), axis=1) for g in range(ngrp)]
    ry = jnp.asarray(np.stack([np.tile(m, (1, 2)) for m in turned]), bf16)
    rz = jnp.asarray(refine_operator(nzc).T, bf16)

    field, saved = theta[0], register[0]
    rows, coarse = velocity.shape[2], planes // 2
    full = jax.ShapeDtypeStruct((planes, ny, nz), f32)
    edge = jax.ShapeDtypeStruct((2 * ny, nz), bf16)
    packed = jax.ShapeDtypeStruct((2 * ny + 4 * rows, nz), bf16)
    vmem = pl.BlockSpec(memory_space=pltpu.VMEM)
    smem = pl.BlockSpec(memory_space=pltpu.SMEM)
    grant = lambda mib: pltpu.CompilerParams(vmem_limit_bytes=mib * 1024 * 1024)

    part = (lax.axis_index("grp") * 2 + lax.axis_index("slab") % 2).astype(jnp.int32)[None]
    out_a, out_b, own = pl.pallas_call(
        pack_kernel,
        out_shape=(packed, packed, jax.ShapeDtypeStruct(velocity.shape, bf16)),
        in_specs=[smem] + [pl.BlockSpec(memory_space=pltpu.HBM)] * 2,
        out_specs=(vmem,) * 3,
        scratch_shapes=[
            pltpu.VMEM((2, ny, nz), f32),
            pltpu.VMEM((2, ny, nz), f32),
            pltpu.SemaphoreType.DMA((3,)),
        ],
        compiler_params=grant(4),
        name="pack",
    )(part, pltpu.with_memory_space_constraint(theta, pltpu.HBM), pltpu.with_memory_space_constraint(velocity, pltpu.HBM))

    def gathered(x):
        turns = [[((i + t) % ngrp, i) for i in range(ngrp)] for t in range(1, ngrp)]
        return [x] + [lax.ppermute(x, "grp", turn) for turn in turns]

    kappa = jnp.broadcast_to(diffusivity[:, None], (8, 128))
    got_a = lax.ppermute(out_a, "slab", swap_a)
    got_b = lax.ppermute(out_b, "slab", swap_b)
    vel = gathered(own)
    gx, halo, out_a, out_b = pl.pallas_call(
        first_kernel,
        out_shape=(full, jax.ShapeDtypeStruct((2, 4 * rows, nz), bf16), edge, edge),
        in_specs=[smem] + [vmem] * 4,
        out_specs=(vmem,) * 4,
        scratch_shapes=[pltpu.VMEM((planes, ny, nz), f32), pltpu.VMEM((4, ny, nz), f32)],
        compiler_params=grant(8),
        name="first",
    )(part, kappa, field, got_a, got_b)
    grad_a = lax.ppermute(out_a, "slab", swap_a)
    grad_b = lax.ppermute(out_b, "slab", swap_b)
    halo = gathered(halo)
    acc, inner = pl.pallas_call(
        functools.partial(inner_kernel, ngrp),
        out_shape=(full, full),
        in_specs=[smem] + [vmem] * (9 + ngrp),
        out_specs=(vmem,) * 2,
        compiler_params=grant(14),
        name="inner",
    )(part, kappa, field, gx, *vel, ky, kz, ky2, kz2, ry, rz)
    new, kept = pl.pallas_call(
        functools.partial(final_kernel, ngrp),
        out_shape=(full, full),
        in_specs=[smem] + [vmem] * (13 + 2 * ngrp),
        out_specs=(pl.BlockSpec(memory_space=pltpu.HBM),) * 2,
        scratch_shapes=[
            pltpu.VMEM((planes, ny, nz), f32),
            pltpu.VMEM((planes, ny, nz), f32),
            pltpu.VMEM((planes + 4, ny, nz), f32),
            pltpu.VMEM((planes, ny, nz), f32),
            pltpu.VMEM((4, ny, nz), f32),
            pltpu.VMEM((4, ny, nz), f32),
            pltpu.SemaphoreType.DMA((2 * planes,)),
        ],
        compiler_params=grant(14),
        name="final",
    )(part, field, saved, acc, inner, gx, got_a, got_b, grad_a, grad_b, *vel, *halo, ky, kz, ry, rz)
    return (new[None], kept[None])


def solution(mesh):
    in_specs = (
        P("grp", "slab", None, None),
        P("grp", "slab", None, None),
        P(None, "slab", "grp", None),
        P("grp"),
    )
    out_specs = (P("grp", "slab", None, None), P("grp", "slab", None, None))
    return jax.shard_map(shards, mesh=mesh, in_specs=in_specs, out_specs=out_specs, check_vma=False)
```
